128 devices in a mesh: group: 2 (over y_hi), tile: 64 (over z, y_lo, x, core).
Axes of the slice: x: 4, y: 4 (y_hi: 2, y_lo: 2; y = y_hi * 2 + y_lo), z: 4, core: 2. Of those that a mesh axis runs over, the one named last changes fastest.
Arguments:
- vorticity: float32 [16, 1024, 1024], P(None, ('group', 'tile')), may hold values from -6 to 6
- layer_to_mode: float32 [16, 16], replicated, may hold values from -1.5 to 1.5
- mode_to_layer: float32 [16, 16], replicated, may hold values from -1.5 to 1.5
- inverse_radii: float32 [16], replicated, may hold values from 0.001 to 1
- wind_curl: float32 [1024, 1024], P(('group', 'tile')), may hold values from -6 to 6
- wet_mask: int32 [1024, 1024], P(('group', 'tile')), may hold values 0 or 1
Outputs:
- new_vorticity: float32 [16, 1024, 1024], P(None, ('group', 'tile'))
- stream: float32 [16, 1024, 1024], P(None, ('group', 'tile'))
The draws below stay inside these ranges and needn't reach their ends.
All inputs are finite; a program needn't handle non-finite values. No bound on the sum of `wet_mask` on one device may be relied on, other than what follows from the above.
Results may differ from the reference program's by a relative error of at most 0.00011.
Values sent between devices are 32-bit elements; how exact they have to be, the bound alone decides.
No kernel may reach another device: no remote copies, remote signals or barrier semaphores. Data moves between devices by JAX's collectives and lax.ppermute only.
A program may use at most 64 MiB of HBM per device.

```python
import math
import jax
import jax.numpy as jnp
from jax import lax

N = 1024
NL = 16


def touch_ends(array, stream_key, low, largest):
    index_at = [jax.random.randint(jax.random.fold_in(stream_key, axis), (), 0, length) for axis, length in enumerate(array.shape)]
    widest = array.shape.index(max(array.shape))
    next_to = index_at[:widest] + [(index_at[widest] + 1) % array.shape[widest]] + index_at[widest + 1:]
    return array.at[tuple(index_at)].set(low).at[tuple(next_to)].set(largest)


def block_scale(key, dims, pieces, smallest, top_value):
    gain = 1.0
    for position, shards_of in pieces:
        heights = jax.random.uniform(jax.random.fold_in(jax.random.fold_in(key, 6), position), (shards_of,), jnp.float32, smallest / len(pieces), top_value / len(pieces))
        gain = gain * jnp.repeat(jnp.exp(heights), dims[position] // shards_of).reshape((-1,) + (1,) * (len(dims) - 1 - position))
    return gain


def centred(stream_key, extent, width, reach, cuts=(), kind=jnp.bfloat16):
    loudness = block_scale(stream_key, extent, cuts, -0.22, 0.18) if cuts else 1.0
    result = jax.random.normal(stream_key, extent, jnp.float32) * width * loudness
    return jnp.minimum(jnp.maximum(result, -reach), reach).astype(kind)


def setup_inputs(seed: int = 0) -> dict:
    key_of = jax.random.split(jax.random.key(seed), 7)
    vorticity = centred(key_of[0], (NL, N, N), 1.0, 6.0, ((1, 128),), jnp.float32)
    layer_to_mode = centred(key_of[1], (NL, NL), NL ** -0.5, 1.5, (), jnp.float32)
    mode_to_layer = centred(key_of[2], (NL, NL), NL ** -0.5, 1.5, (), jnp.float32)
    inverse_radii = jnp.clip(jnp.exp(jax.random.uniform(key_of[3], (NL,), jnp.float32, math.log(0.001), math.log(1.0))), 0.001, 1.0)
    wind_curl = centred(key_of[4], (N, N), 1.0, 6.0, ((0, 128),), jnp.float32)
    wet_mask = touch_ends((jax.random.randint(key_of[5], (N, N), 0, 10) < 9).astype(jnp.int32), jax.random.fold_in(key_of[5], 1), 0, 1)
    return {"vorticity": vorticity, "layer_to_mode": layer_to_mode, "mode_to_layer": mode_to_layer, "inverse_radii": inverse_radii, "wind_curl": wind_curl, "wet_mask": wet_mask}


time_step = 0.5
beta_plane = 1.0
bottom_drag = 0.2

def make_table(length, positions):
    wavenumber = jnp.arange(length, dtype=jnp.int32) + 1
    phase_index = wavenumber[:, None] * (positions[None, :] + 1) % (2 * (length + 1))
    return math.sqrt(2.0 / (length + 1)) * jnp.sin(math.pi * phase_index.astype(jnp.float32) / (length + 1))

def eigen_values(length, positions):
    return 4.0 * jnp.sin(math.pi * (positions + 1).astype(jnp.float32) / (2 * (length + 1))) ** 2

def matmul(matrix, operand):
    return jnp.dot(matrix, operand, precision=lax.Precision.HIGHEST, preferred_element_type=jnp.float32)

def offset_view(padded, row_step, column_step):
    height = padded.shape[1] - 2
    breadth = padded.shape[2] - 2
    return padded[:, 1 + row_step:1 + row_step + height, 1 + column_step:1 + column_step + breadth]

def tendency_of(vortex_pad, stream_pad, wind_curl):
    vortex_north = offset_view(vortex_pad, 1, 0)
    vortex_south = offset_view(vortex_pad, -1, 0)
    vortex_east = offset_view(vortex_pad, 0, 1)
    vortex_west = offset_view(vortex_pad, 0, -1)
    vortex_northeast = offset_view(vortex_pad, 1, 1)
    vortex_northwest = offset_view(vortex_pad, 1, -1)
    vortex_southeast = offset_view(vortex_pad, -1, 1)
    vortex_southwest = offset_view(vortex_pad, -1, -1)
    stream_mid = offset_view(stream_pad, 0, 0)
    stream_north = offset_view(stream_pad, 1, 0)
    stream_south = offset_view(stream_pad, -1, 0)
    stream_east = offset_view(stream_pad, 0, 1)
    stream_west = offset_view(stream_pad, 0, -1)
    stream_northeast = offset_view(stream_pad, 1, 1)
    stream_northwest = offset_view(stream_pad, 1, -1)
    stream_southeast = offset_view(stream_pad, -1, 1)
    stream_southwest = offset_view(stream_pad, -1, -1)
    arakawa_one = (stream_east - stream_west) * (vortex_north - vortex_south) - (stream_north - stream_south) * (vortex_east - vortex_west)
    arakawa_two = stream_east * (vortex_northeast - vortex_southeast) - stream_west * (vortex_northwest - vortex_southwest) - stream_north * (vortex_northeast - vortex_northwest) + stream_south * (vortex_southeast - vortex_southwest)
    arakawa_three = vortex_north * (stream_northeast - stream_northwest) - vortex_south * (stream_southeast - stream_southwest) - vortex_east * (stream_northeast - stream_southeast) + vortex_west * (stream_northwest - stream_southwest)
    jacobian = (arakawa_one + arakawa_two + arakawa_three) / 12.0
    laplace = stream_north + stream_south + stream_east + stream_west - 4.0 * stream_mid
    layers = stream_mid.shape[0]
    layer_index = jnp.arange(layers, dtype=jnp.int32)
    top_layer = (layer_index == 0).astype(jnp.float32)[:, None, None]
    bottom_layer = (layer_index == layers - 1).astype(jnp.float32)[:, None, None]
    return -jacobian - beta_plane * 0.5 * (stream_east - stream_west) + top_layer * wind_curl[None] - bottom_drag * bottom_layer * laplace

def reference(vorticity, layer_to_mode, mode_to_layer, inverse_radii, wind_curl, wet_mask):
    length = vorticity.shape[-1]
    positions = jnp.arange(length, dtype=jnp.int32)
    sine = make_table(length, positions)
    eigens = eigen_values(length, positions)
    modal_field = jnp.einsum('ml,lyx->myx', layer_to_mode, vorticity, precision=lax.Precision.HIGHEST)

    def invert(operands):
        plane_field, radius = operands
        spectrum = matmul(matmul(sine, plane_field), sine)
        spectrum = -spectrum / (eigens[:, None] + eigens[None, :] + radius)
        return matmul(matmul(sine, spectrum), sine)
    stream_modes = lax.map(invert, (modal_field, inverse_radii))
    stream = jnp.einsum('lm,myx->lyx', mode_to_layer, stream_modes, precision=lax.Precision.HIGHEST)
    padding = ((0, 0), (1, 1), (1, 1))
    tendency = tendency_of(jnp.pad(vorticity, padding), jnp.pad(stream, padding), wind_curl)
    return (vorticity + time_step * wet_mask.astype(jnp.float32) * tendency, stream)
```

```python
import functools
import math

import jax
import jax.numpy as jnp
import numpy as np
from jax import lax
from jax.experimental import pallas as pl
from jax.experimental.pallas import tpu as pltpu
from jax.sharding import PartitionSpec as P

time_step = 0.5
beta_plane = 1.0
bottom_drag = 0.2

N = 1024
NL = 16
ROWS = 8
BLOCKS = 128
LANES = 128
AXES = ("group", "tile")
HIGHEST = lax.Precision.HIGHEST
VMEM = pl.BlockSpec(memory_space=pltpu.VMEM)
SMEM = pl.BlockSpec(memory_space=pltpu.SMEM)


def host_tables():
    k = np.arange(1, N + 1)
    a = 32 * np.arange(32)
    b = np.arange(1, 33)
    turn = 2 * (N + 1)
    angle_a = np.pi * ((a[:, None] * k[None, :]) % turn) / (N + 1)
    angle_b = np.pi * ((b[:, None] * k[None, :]) % turn) / (N + 1)
    scale = math.sqrt(2.0 / (N + 1))
    eigen = 4.0 * np.sin(np.pi * k / (2 * (N + 1))) ** 2
    return [
        np.asarray(t, np.float32)
        for t in (
            np.sin(angle_a),
            np.cos(angle_a),
            scale * np.sin(angle_b),
            scale * np.cos(angle_b),
            eigen,
        )
    ]


def iota(shape, dim):
    return lax.broadcasted_iota(jnp.int32, shape, dim)


def dot(left, right, precision=None):
    return lax.dot_general(
        left,
        right,
        (((1,), (0,)), ((), ())),
        precision=precision,
        preferred_element_type=jnp.float32,
    )


def halves(value):
    high = value.astype(jnp.bfloat16)
    low = (value - high.astype(jnp.float32)).astype(jnp.bfloat16)
    return high, low


def radii_column(radii_ref, shape):
    sub = iota(shape, 0)
    column = jnp.zeros(shape, jnp.float32)
    for m in range(NL):
        column = jnp.where(sub == m, radii_ref[m], column)
    return column


def decay_of(shift):
    half = 0.5 * jnp.sqrt(shift)
    root = jnp.sqrt(1.0 + 0.25 * shift)
    grow = half + root
    return 1.0 / (grow * grow), 1.0 / (4.0 * half * root)


def transform(rows, table_high, table_low):
    high, low = rows
    count = high.shape[0]
    both = dot(jnp.concatenate([high, low], 0), table_high)
    return both[:count] + both[count:] + dot(high, table_low)


def forward_kernel(
    vortex_ref, mix_ref, radii_ref, eigen_ref, sa_ref, ca_ref, sb_ref, cb_ref,
    send_ref, force_ref, high_ref, low_ref,
):
    rows = NL * ROWS
    spread = (iota((NL, rows), 1) // ROWS == iota((NL, rows), 0)).astype(jnp.float32)
    wide = dot(mix_ref[...], spread, HIGHEST)
    mix = jnp.concatenate([wide] * ROWS, 0)
    mix = jnp.where(iota((rows, rows), 0) // NL == iota((rows, rows), 1) % ROWS, mix, 0.0)
    modal = dot(mix, vortex_ref[...].reshape(rows, N), HIGHEST)
    split = halves(modal)
    rho, weight = decay_of(eigen_ref[...].reshape(1, N) + radii_column(radii_ref, (NL, N)))
    step = 256
    for n in range(N // step):
        cols = slice(n * step, (n + 1) * step)
        for a in range(32):
            block = sa_ref[a : a + 1, cols] * cb_ref[:, cols] + ca_ref[a : a + 1, cols] * sb_ref[:, cols]
            high, low = halves(block)
            high_ref[32 * a : 32 * a + 32, cols] = high
            low_ref[32 * a : 32 * a + 32, cols] = low
        spectrum = transform(split, high_ref[:, cols], low_ref[:, cols])
        right = jnp.zeros((NL, step), jnp.float32)
        left = jnp.zeros((NL, step), jnp.float32)
        force = []
        for y in range(ROWS):
            force.append(-weight[:, cols] * spectrum[y * NL : (y + 1) * NL])
            force_ref[y, :, cols] = force[y]
            right = rho[:, cols] * right + force[y]
        for y in reversed(range(ROWS)):
            left = rho[:, cols] * left + force[y]
        for c in range(step // LANES):
            dest = n * (step // LANES) + c
            part = slice(c * LANES, (c + 1) * LANES)
            send_ref[dest * NL : (dest + 1) * NL, 0, :LANES] = right[:, part]
            send_ref[dest * NL : (dest + 1) * NL, 0, LANES:] = left[:, part]


def shift_rows(value, step):
    blank = jnp.zeros((abs(step), value.shape[1]), value.dtype)
    if step > 0:
        return jnp.concatenate([blank, value[:-step]], 0)
    return jnp.concatenate([value[-step:], blank], 0)


def scan_kernel(index_ref, radii_ref, eigen_ref, take_ref, give_ref):
    me = index_ref[0]
    mode = me % NL
    chunk = me // NL
    shift = eigen_ref[pl.ds(chunk, 1), :] + radii_ref[mode]
    rho, _ = decay_of(shift)
    rho2 = rho * rho
    rho4 = rho2 * rho2
    block = rho4 * rho4
    right = take_ref[:, 0, :LANES]
    left = take_ref[:, 0, LANES:]
    place = iota((BLOCKS, LANES), 0)
    power = jnp.ones((BLOCKS, LANES), jnp.float32)
    rate = block
    step = 1
    while step < BLOCKS:
        right = right + rate * shift_rows(right, step)
        left = left + rate * shift_rows(left, -step)
        power = jnp.where((place // step) % 2 == 1, power * rate, power)
        rate = rate * rate
        step *= 2
    below = rho * left[:1]
    above = rho * right[BLOCKS - 1 :]
    far = rate * rho
    scale = 1.0 / (1.0 - far * far)
    alpha = -(below - far * above) * scale
    beta = -(above - far * below) * scale
    back = jnp.where(place == BLOCKS - 1, 1.0, 0.0)
    reverse = jnp.ones((BLOCKS, LANES), jnp.float32)
    rate = block
    step = 1
    while step < BLOCKS:
        reverse = jnp.where(((BLOCKS - 1 - place) // step) % 2 == 1, reverse * rate, reverse)
        rate = rate * rate
        step *= 2
    give_ref[:, 0, :LANES] = shift_rows(right, 1) + alpha * power
    give_ref[:, 0, LANES:] = shift_rows(left, -1) + beta * reverse


def roll_lanes(value, step):
    width = value.shape[1]
    lane = iota(value.shape, 1)
    rolled = pltpu.roll(value, step % width, 1)
    return jnp.where(lane == (0 if step > 0 else width - 1), 0.0, rolled)


def roll_sub(value, edge, step):
    height = value.shape[0]
    sub = iota(value.shape, 0)
    rolled = pltpu.roll(value, step % height, 0)
    return jnp.where(sub == (0 if step > 0 else height - 1), edge, rolled)


def local_kernel(
    force_ref, vortex_ref, south_ref, north_ref, wind_ref, wet_ref, radii_ref, eigen_ref, mix_ref,
    part_ref, mixed_ref, base_ref, coef_ref, drag_ref,
):
    rho, _ = decay_of(eigen_ref[...].reshape(1, N) + radii_column(radii_ref, (NL, N)))
    right = jnp.zeros((NL, N), jnp.float32)
    for y in range(ROWS):
        right = rho * right + force_ref[y]
        part_ref[y + 1] = right
    part_ref[ROWS + 1] = rho * right
    left = jnp.zeros((NL, N), jnp.float32)
    for y in reversed(range(ROWS)):
        part_ref[y + 1] += left
        left = rho * (left + force_ref[y])
    part_ref[0] = left
    tall = NL * (ROWS + 2)
    row = iota((tall, NL), 0)
    layer = jnp.where(row < NL * ROWS, row // ROWS, row % NL)
    pick = (layer == iota((tall, NL), 1)).astype(jnp.float32)
    wide = (iota((NL, tall), 1) % NL == iota((NL, tall), 0)).astype(jnp.float32)
    mixed = dot(dot(pick, mix_ref[...], HIGHEST), wide, HIGHEST)
    row = iota((tall, tall), 0)
    place = jnp.where(row < NL * ROWS, row % ROWS + 1, jnp.where(row < NL * (ROWS + 1), 0, ROWS + 1))
    mixed_ref[...] = jnp.where(iota((tall, tall), 1) // NL == place, mixed, 0.0)
    keep = time_step * wet_ref[...].astype(jnp.float32)
    twelfth = keep * (1.0 / 12.0)
    for layer in range(NL):
        mid = vortex_ref[layer]
        north = roll_sub(mid, north_ref[layer : layer + 1], -1)
        south = roll_sub(mid, south_ref[layer : layer + 1], 1)
        east = roll_lanes(mid, -1)
        west = roll_lanes(mid, 1)
        north_east = roll_lanes(north, -1)
        north_west = roll_lanes(north, 1)
        south_east = roll_lanes(south, -1)
        south_west = roll_lanes(south, 1)
        along = north - south
        across = east - west
        c_east = -twelfth * (along + (north_east - south_east)) - keep * (0.5 * beta_plane)
        c_west = twelfth * (along + (north_west - south_west)) + keep * (0.5 * beta_plane)
        c_north = twelfth * (across + (north_east - north_west))
        c_south = -twelfth * (across + (south_east - south_west))
        if layer == NL - 1:
            drag = keep * bottom_drag
            c_east = c_east - drag
            c_west = c_west - drag
            c_north = c_north - drag
            c_south = c_south - drag
            drag_ref[...] = 4.0 * drag
        coef_ref[0, layer] = c_north
        coef_ref[1, layer] = c_south
        coef_ref[2, layer] = roll_lanes(c_east, 1)
        coef_ref[3, layer] = roll_lanes(-twelfth * (north - east), 1)
        coef_ref[4, layer] = roll_lanes(twelfth * (south - east), 1)
        coef_ref[5, layer] = roll_lanes(c_west, -1)
        coef_ref[6, layer] = roll_lanes(twelfth * (north - west), -1)
        coef_ref[7, layer] = roll_lanes(-twelfth * (south - west), -1)
        base_ref[layer] = mid + keep * wind_ref[...] if layer == 0 else mid


def backward_kernel(
    index_ref, take_ref, part_ref, radii_ref, eigen_ref, high_ref, low_ref, mixed_ref, base_ref, coef_ref, drag_ref,
    vortex_ref, stream_ref, psi_ref, wave_ref,
):
    tall = NL * (ROWS + 2)
    rho, _ = decay_of(eigen_ref[...].reshape(1, N) + radii_column(radii_ref, (NL, N)))
    for c in range(N // LANES):
        cols = slice(c * LANES, (c + 1) * LANES)
        up = take_ref[c * NL : (c + 1) * NL, 0, :LANES]
        down = take_ref[c * NL : (c + 1) * NL, 0, LANES:]
        near = rho[:, cols]
        ups, downs = [up], [down]
        for _ in range(ROWS + 1):
            ups.append(ups[-1] * near)
            downs.append(downs[-1] * near)
        for i in range(ROWS + 2):
            psi_ref[i * NL : (i + 1) * NL, cols] = part_ref[i, :, cols] + ups[i] + downs[ROWS + 1 - i]
    split = halves(dot(mixed_ref[...], psi_ref[...], HIGHEST))
    step = 256
    for n in range(N // step):
        cols = slice(n * step, (n + 1) * step)
        wave_ref[:, cols] = transform(split, high_ref[:, cols], low_ref[:, cols])
    inside_low = jnp.where(index_ref[0] > 0, 1.0, 0.0)
    inside_high = jnp.where(index_ref[0] < BLOCKS - 1, 1.0, 0.0)
    body = NL * ROWS
    for layer in range(NL):
        mid = wave_ref[layer * ROWS : (layer + 1) * ROWS]
        north = roll_sub(mid, inside_high * wave_ref[body + NL + layer : body + NL + layer + 1], -1)
        south = roll_sub(mid, inside_low * wave_ref[body + layer : body + layer + 1], 1)
        stream_ref[layer] = mid
        total = base_ref[layer] + coef_ref[0, layer] * north + coef_ref[1, layer] * south
        if layer == NL - 1:
            total = total + drag_ref[...] * mid
        from_east = coef_ref[2, layer] * mid + coef_ref[3, layer] * north + coef_ref[4, layer] * south
        from_west = coef_ref[5, layer] * mid + coef_ref[6, layer] * north + coef_ref[7, layer] * south
        total = total + pltpu.roll(from_east, N - 1, 1) + pltpu.roll(from_west, 1, 1)
        vortex_ref[layer] = total


def call(kernel, outs, specs, args, flops, nbytes, scratch=(), limit=24 << 20):
    return pl.pallas_call(
        kernel,
        out_shape=[jax.ShapeDtypeStruct(s, d) for s, d in outs],
        in_specs=specs,
        out_specs=[VMEM] * len(outs),
        scratch_shapes=list(scratch),
        compiler_params=pltpu.CompilerParams(vmem_limit_bytes=limit),
        cost_estimate=pl.CostEstimate(flops=flops, bytes_accessed=nbytes, transcendentals=0),
    )(*args)


def body(vorticity, layer_to_mode, mode_to_layer, inverse_radii, wind_curl, wet_mask):
    f32, bf16 = jnp.float32, jnp.bfloat16
    sin_a, cos_a, sin_b, cos_b, eigen = (jnp.asarray(t) for t in host_tables())
    eigen = eigen.reshape(N // LANES, LANES)
    index = (lax.axis_index("group") * lax.axis_size("tile") + lax.axis_index("tile")).astype(jnp.int32).reshape(1)
    south = lax.ppermute(vorticity[:, ROWS - 1], AXES, [(i, i + 1) for i in range(BLOCKS - 1)])
    north = lax.ppermute(vorticity[:, 0], AXES, [(i + 1, i) for i in range(BLOCKS - 1)])
    eigen_row = eigen.reshape(1, N)
    send, force, high, low = call(
        forward_kernel,
        [((BLOCKS, 1, 2 * LANES), f32), ((ROWS, NL, N), f32), ((N, N), bf16), ((N, N), bf16)],
        [VMEM, VMEM, SMEM] + [VMEM] * 5,
        (vorticity, layer_to_mode, inverse_radii, eigen_row, sin_a, cos_a, sin_b, cos_b),
        6 * 2 * 128 * N * N, 8 << 20,
    )
    take = lax.all_to_all(send, AXES, split_axis=0, concat_axis=0, tiled=True)
    part, mixed, base, coef, drag = call(
        local_kernel,
        [((ROWS + 2, NL, N), f32), ((160, 160), f32), ((NL, ROWS, N), f32), ((8, NL, ROWS, N), f32), ((ROWS, N), f32)],
        [VMEM] * 6 + [SMEM] + [VMEM] * 2,
        (force, vorticity, south, north, wind_curl, wet_mask, inverse_radii, eigen_row, mode_to_layer),
        1 << 27, 8 << 20,
    )
    (give,) = call(
        scan_kernel,
        [((BLOCKS, 1, 2 * LANES), f32)],
        [SMEM, SMEM, VMEM, VMEM],
        (index, inverse_radii, eigen, take),
        1 << 20, 1 << 18,
    )
    amplitude = lax.all_to_all(give, AXES, split_axis=0, concat_axis=0, tiled=True)
    new_vorticity, stream = call(
        backward_kernel,
        [((NL, ROWS, N), f32), ((NL, ROWS, N), f32)],
        [SMEM, VMEM, VMEM, SMEM] + [VMEM] * 7,
        (index, amplitude, part, inverse_radii, eigen_row, high, low, mixed, base, coef, drag),
        6 * 2 * 160 * N * N, 10 << 20,
        scratch=(pltpu.VMEM((160, N), f32), pltpu.VMEM((160, N), f32)),
    )
    return new_vorticity, stream


def solution(mesh):
    rows = P(None, AXES, None)
    return jax.shard_map(
        body,
        mesh=mesh,
        in_specs=(rows, P(), P(), P(), P(AXES, None), P(AXES, None)),
        out_specs=(rows, rows),
        check_vma=False,
    )
```

```python
import math

import jax
import jax.numpy as jnp
import numpy as np
from jax import lax
from jax.experimental import pallas as pl
from jax.experimental.pallas import tpu as pltpu
from jax.sharding import PartitionSpec as P

time_step = 0.5
beta_plane = 1.0
bottom_drag = 0.2

N = 1024
NL = 16
ROWS = 8
TALL = ROWS + 2
BLOCKS = 128
LANES = 128
STEP = 256
PIECES = N // STEP
AXES = ("group", "tile")
HIGHEST = lax.Precision.HIGHEST
SMEM = pl.BlockSpec(memory_space=pltpu.SMEM)
ANY = pl.BlockSpec(memory_space=pl.ANY)
DMA = pltpu.SemaphoreType.DMA
f32, bf16, i32 = jnp.float32, jnp.bfloat16, jnp.int32


def host_table():
    k = np.arange(1, N + 1)
    turn = 2 * (N + 1)
    angle_a = np.pi * ((32 * np.arange(32)[:, None] * k[None, :]) % turn) / (N + 1)
    angle_b = np.pi * ((np.arange(1, 33)[:, None] * k[None, :]) % turn) / (N + 1)
    scale = math.sqrt(2.0 / (N + 1))
    table = [np.sin(angle_a), np.cos(angle_a), scale * np.sin(angle_b), scale * np.cos(angle_b)]
    return np.stack(table).astype(np.float32)


def iota(shape, dim):
    return lax.broadcasted_iota(jnp.int32, shape, dim)


def dot(left, right, precision=None):
    return lax.dot_general(
        left, right, (((1,), (0,)), ((), ())), precision=precision, preferred_element_type=jnp.float32
    )


def halves(value):
    high = value.astype(jnp.bfloat16)
    low = (value - high.astype(jnp.float32)).astype(jnp.bfloat16)
    return high, low


def split_dot(left, right):
    count = left[0].shape[0]
    both = dot(jnp.concatenate(left, 0), right[0])
    return both[:count] + both[count:] + dot(left[0], right[1])


def fetch(pairs, sems, first=0):
    copies = [pltpu.make_async_copy(src, dst, sems.at[first + i]) for i, (src, dst) in enumerate(pairs)]
    for copy in copies:
        copy.start()
    return copies


def wait(copies):
    for copy in copies:
        copy.wait()


def eigen_values(first, width):
    wave = (iota((1, width), 1) + (first + 1)).astype(jnp.float32)
    angle = wave * (math.pi / (2 * (N + 1)))
    square = angle * angle
    series = jnp.full_like(square, 1.0 / math.factorial(15))
    for order in (13, 11, 9, 7, 5, 3, 1):
        series = 1.0 / math.factorial(order) - square * series
    sine = angle * series
    return 4.0 * sine * sine


def radii_column(radii_ref, shape):
    sub = iota(shape, 0)
    column = jnp.zeros(shape, jnp.float32)
    for m in range(NL):
        column = jnp.where(sub == m, radii_ref[m], column)
    return column


def decay_of(shift):
    half = 0.5 * jnp.sqrt(shift)
    root = jnp.sqrt(1.0 + 0.25 * shift)
    grow = half + root
    return 1.0 / (grow * grow), 1.0 / (4.0 * half * root)


def mode_decay(radii_ref):
    return decay_of(eigen_values(0, N) + radii_column(radii_ref, (NL, N)))


def forward_kernel(
    vortex_hbm, mix_hbm, radii_hbm, table_hbm,
    send_hbm, force_hbm, first_hbm, last_hbm, high_hbm, low_hbm,
    vortex_ref, mix_ref, radii_ref, table_ref,
    send_ref, force_ref, first_ref, last_ref, high_ref, low_ref, sems,
):
    copies = fetch(
        [(mix_hbm, mix_ref), (radii_hbm, radii_ref), (vortex_hbm, vortex_ref), (table_hbm, table_ref)], sems
    )
    rows = NL * ROWS
    spread = (iota((NL, rows), 1) // ROWS == iota((NL, rows), 0)).astype(jnp.float32)
    wait(copies[:2])
    rho, weight = mode_decay(radii_ref)
    wide = dot(mix_ref[...], spread, HIGHEST)
    mix = jnp.concatenate([wide] * ROWS, 0)
    mix = jnp.where(iota((rows, rows), 0) // NL == iota((rows, rows), 1) % ROWS, mix, 0.0)
    wait(copies[2:3])
    first_ref[...] = vortex_ref[:, 0]
    last_ref[...] = vortex_ref[:, ROWS - 1]
    written = fetch([(first_ref, first_hbm), (last_ref, last_hbm)], sems, 4)
    modal = split_dot(halves(mix), halves(vortex_ref[...].reshape(rows, N)))
    split = halves(modal)
    wait(copies[3:])
    for n in range(PIECES):
        cols = slice(n * STEP, (n + 1) * STEP)
        for a in range(32):
            block = table_ref[0, a : a + 1, cols] * table_ref[3, :, cols]
            block += table_ref[1, a : a + 1, cols] * table_ref[2, :, cols]
            high, low = halves(block)
            high_ref[n, 32 * a : 32 * a + 32] = high
            low_ref[n, 32 * a : 32 * a + 32] = low
        written += fetch([(high_ref.at[n], high_hbm.at[n]), (low_ref.at[n], low_hbm.at[n])], sems, 6 + 3 * n)
        spectrum = split_dot(split, (high_ref[n], low_ref[n]))
        right = jnp.zeros((NL, STEP), jnp.float32)
        left = jnp.zeros((NL, STEP), jnp.float32)
        force = []
        for y in range(ROWS):
            force.append(-weight[:, cols] * spectrum[y * NL : (y + 1) * NL])
            force_ref[y, :, cols] = force[y]
            right = rho[:, cols] * right + force[y]
        for y in reversed(range(ROWS)):
            left = rho[:, cols] * left + force[y]
        for c in range(STEP // LANES):
            dest = n * (STEP // LANES) + c
            part = slice(c * LANES, (c + 1) * LANES)
            send_ref[dest * NL : (dest + 1) * NL, 0, :LANES] = right[:, part]
            send_ref[dest * NL : (dest + 1) * NL, 0, LANES:] = left[:, part]
        dests = pl.ds(n * (STEP // LANES) * NL, STEP // LANES * NL)
        written += fetch([(send_ref.at[dests], send_hbm.at[dests])], sems, 8 + 3 * n)
    written += fetch([(force_ref, force_hbm)], sems, 6 + 3 * PIECES)
    wait(written)


def shift_rows(value, step):
    blank = jnp.zeros((abs(step), value.shape[1]), value.dtype)
    if step > 0:
        return jnp.concatenate([blank, value[:-step]], 0)
    return jnp.concatenate([value[-step:], blank], 0)


def scan_kernel(
    index_ref, radii_hbm, take_hbm, after_hbm, first_hbm, last_hbm, give_hbm, radii_ref, take_ref, give_ref, sems
):
    del after_hbm, first_hbm, last_hbm
    copies = fetch([(radii_hbm, radii_ref), (take_hbm, take_ref)], sems)
    copies[0].wait()
    me = index_ref[0]
    rho, _ = decay_of(eigen_values(me // NL * LANES, LANES) + radii_ref[me % NL])
    rho2 = rho * rho
    rho4 = rho2 * rho2
    place = iota((BLOCKS, LANES), 0)
    rates = [rho4 * rho4]
    while 2 ** len(rates) <= BLOCKS:
        rates.append(rates[-1] * rates[-1])
    power = jnp.ones((BLOCKS, LANES), jnp.float32)
    reverse = power
    for bit, rate in enumerate(rates[:-1]):
        odd = (place >> bit) % 2 == 1
        power = power * jnp.where(odd, rate, 1.0)
        reverse = reverse * jnp.where(odd, 1.0, rate)
    copies[1].wait()
    right = take_ref[:, 0, :LANES]
    left = take_ref[:, 0, LANES:]
    for bit, rate in enumerate(rates[:-1]):
        right = right + rate * shift_rows(right, 1 << bit)
        left = left + rate * shift_rows(left, -1 << bit)
    below = rho * left[:1]
    above = rho * right[BLOCKS - 1 :]
    far = rates[-1] * rho
    scale = 1.0 / (1.0 - far * far)
    alpha = -(below - far * above) * scale
    beta = -(above - far * below) * scale
    give_ref[:, 0, :LANES] = shift_rows(right, 1) + alpha * power
    give_ref[:, 0, LANES:] = shift_rows(left, -1) + beta * reverse
    wait(fetch([(give_ref, give_hbm)], sems))


def part_kernel(
    force_hbm, radii_hbm, mix_hbm, part_hbm, mixed_hbm, force_ref, radii_ref, mix_ref, part_ref, mixed_ref, sems
):
    copies = fetch([(radii_hbm, radii_ref), (mix_hbm, mix_ref), (force_hbm, force_ref)], sems)
    wait(copies[:2])
    tall = NL * TALL
    row = iota((tall, NL), 0)
    layer = jnp.where(row < NL * ROWS, row // ROWS, row % NL)
    pick = (layer == iota((tall, NL), 1)).astype(jnp.float32)
    wide = (iota((NL, tall), 1) % NL == iota((NL, tall), 0)).astype(jnp.float32)
    mixed = dot(dot(pick, mix_ref[...], HIGHEST), wide, HIGHEST)
    row = iota((tall, tall), 0)
    place = jnp.where(row < NL * ROWS, row % ROWS + 1, jnp.where(row < NL * (ROWS + 1), 0, ROWS + 1))
    mixed_ref[...] = jnp.where(iota((tall, tall), 1) // NL == place, mixed, 0.0)
    written = fetch([(mixed_ref, mixed_hbm)], sems, 3)
    rho, _ = mode_decay(radii_ref)
    wait(copies[2:])
    right = jnp.zeros((NL, N), jnp.float32)
    for y in range(ROWS):
        right = rho * right + force_ref[y]
        part_ref[y + 1] = right
    part_ref[ROWS + 1] = rho * right
    left = jnp.zeros((NL, N), jnp.float32)
    for y in reversed(range(ROWS)):
        part_ref[y + 1] += left
        left = rho * (left + force_ref[y])
    part_ref[0] = left
    wait(written + fetch([(part_ref, part_hbm)], sems, 4))


def roll_lanes(value, step):
    width = value.shape[1]
    lane = iota(value.shape, 1)
    rolled = pltpu.roll(value, step % width, 1)
    return jnp.where(lane == (0 if step > 0 else width - 1), 0.0, rolled)


def roll_sub(value, edge, step):
    height = value.shape[0]
    sub = iota(value.shape, 0)
    rolled = pltpu.roll(value, step % height, 0)
    return jnp.where(sub == (0 if step > 0 else height - 1), edge, rolled)


def weight_kernel(
    vortex_hbm, wind_hbm, wet_hbm, south_hbm, north_hbm, after_hbm, base_hbm, coef_hbm, drag_hbm,
    vortex_ref, wind_ref, wet_ref, south_ref, north_ref, base_ref, coef_ref, drag_ref, sems,
):
    del after_hbm
    wait(
        fetch(
            [
                (wet_hbm, wet_ref), (wind_hbm, wind_ref), (south_hbm, south_ref), (north_hbm, north_ref),
                (vortex_hbm, vortex_ref),
            ],
            sems,
        )
    )
    keep = time_step * wet_ref[...].astype(jnp.float32)
    twelfth = keep * (1.0 / 12.0)
    written = []
    for layer in range(NL):
        mid = vortex_ref[layer]
        north = roll_sub(mid, north_ref[layer : layer + 1], -1)
        south = roll_sub(mid, south_ref[layer : layer + 1], 1)
        east = roll_lanes(mid, -1)
        west = roll_lanes(mid, 1)
        north_east = roll_lanes(north, -1)
        north_west = roll_lanes(north, 1)
        south_east = roll_lanes(south, -1)
        south_west = roll_lanes(south, 1)
        along = north - south
        across = east - west
        c_east = -twelfth * (along + (north_east - south_east)) - keep * (0.5 * beta_plane)
        c_west = twelfth * (along + (north_west - south_west)) + keep * (0.5 * beta_plane)
        c_north = twelfth * (across + (north_east - north_west))
        c_south = -twelfth * (across + (south_east - south_west))
        if layer == NL - 1:
            drag = keep * bottom_drag
            c_east = c_east - drag
            c_west = c_west - drag
            c_north = c_north - drag
            c_south = c_south - drag
            drag_ref[...] = 4.0 * drag
        coef_ref[layer, 0] = c_north
        coef_ref[layer, 1] = c_south
        coef_ref[layer, 2] = roll_lanes(c_east, 1)
        coef_ref[layer, 3] = roll_lanes(-twelfth * (north - east), 1)
        coef_ref[layer, 4] = roll_lanes(twelfth * (south - east), 1)
        coef_ref[layer, 5] = roll_lanes(c_west, -1)
        coef_ref[layer, 6] = roll_lanes(twelfth * (north - west), -1)
        coef_ref[layer, 7] = roll_lanes(-twelfth * (south - west), -1)
        base_ref[layer] = mid + keep * wind_ref[...] if layer == 0 else mid
        if layer % 4 == 3:
            some = pl.ds(layer - 3, 4)
            written += fetch([(coef_ref.at[some], coef_hbm.at[some])], sems, 5 + layer // 4)
    wait(written + fetch([(base_ref, base_hbm), (drag_ref, drag_hbm)], sems, 9))


def backward_kernel(
    index_ref, radii_hbm, take_hbm, part_hbm, mixed_hbm, high_hbm, low_hbm, base_hbm, coef_hbm, drag_hbm,
    vortex_hbm, stream_hbm,
    radii_ref, take_ref, part_ref, mixed_ref, high_ref, low_ref, base_ref, coef_ref, drag_ref,
    psi_ref, wave_ref, vortex_ref, stream_ref, sems,
):
    copies = fetch(
        [
            (radii_hbm, radii_ref), (take_hbm, take_ref), (part_hbm, part_ref), (mixed_hbm, mixed_ref),
            (high_hbm, high_ref), (low_hbm, low_ref), (coef_hbm, coef_ref), (base_hbm, base_ref),
            (drag_hbm, drag_ref),
        ],
        sems,
    )
    out = len(copies)
    copies[0].wait()
    rho, _ = mode_decay(radii_ref)
    wait(copies[1:3])
    for c in range(N // LANES):
        cols = slice(c * LANES, (c + 1) * LANES)
        up = take_ref[c * NL : (c + 1) * NL, 0, :LANES]
        down = take_ref[c * NL : (c + 1) * NL, 0, LANES:]
        near = rho[:, cols]
        ups, downs = [up], [down]
        for _ in range(ROWS + 1):
            ups.append(ups[-1] * near)
            downs.append(downs[-1] * near)
        for i in range(TALL):
            psi_ref[i * NL : (i + 1) * NL, cols] = part_ref[i, :, cols] + ups[i] + downs[ROWS + 1 - i]
    wait(copies[3:4])
    split = halves(split_dot(halves(mixed_ref[...]), halves(psi_ref[...])))
    wait(copies[4:6])
    for n in range(PIECES):
        wave_ref[:, n * STEP : (n + 1) * STEP] = split_dot(split, (high_ref[n], low_ref[n]))
    inside_low = jnp.where(index_ref[0] > 0, 1.0, 0.0)
    inside_high = jnp.where(index_ref[0] < BLOCKS - 1, 1.0, 0.0)
    body = NL * ROWS
    for layer in range(NL):
        stream_ref[layer] = wave_ref[layer * ROWS : (layer + 1) * ROWS]
    written = fetch([(stream_ref, stream_hbm)], sems, out)
    wait(copies[6:])
    for layer in range(NL):
        mid = wave_ref[layer * ROWS : (layer + 1) * ROWS]
        north = roll_sub(mid, inside_high * wave_ref[body + NL + layer : body + NL + layer + 1], -1)
        south = roll_sub(mid, inside_low * wave_ref[body + layer : body + layer + 1], 1)
        total = base_ref[layer] + coef_ref[layer, 0] * north + coef_ref[layer, 1] * south
        if layer == NL - 1:
            total = total + drag_ref[...] * mid
        from_east = coef_ref[layer, 2] * mid + coef_ref[layer, 3] * north + coef_ref[layer, 4] * south
        from_west = coef_ref[layer, 5] * mid + coef_ref[layer, 6] * north + coef_ref[layer, 7] * south
        vortex_ref[layer] = total + pltpu.roll(from_east, N - 1, 1) + pltpu.roll(from_west, 1, 1)
        if layer % 4 == 3:
            some = pl.ds(layer - 3, 4)
            written += fetch([(vortex_ref.at[some], vortex_hbm.at[some])], sems, out + 1 + layer // 4)
    wait(written)


def call(kernel, outs, args, scratch, flops, nbytes, index=None, limit=60 * 1024 * 1024):
    def room(kind):
        return pltpu.VMEM(*kind) if isinstance(kind, tuple) else kind

    lead = [] if index is None else [index]
    return pl.pallas_call(
        kernel,
        out_shape=[jax.ShapeDtypeStruct(s, d) for s, d in outs],
        in_specs=[SMEM] * len(lead) + [ANY] * len(args),
        out_specs=[ANY] * len(outs),
        scratch_shapes=[room(kind) for kind in scratch],
        compiler_params=pltpu.CompilerParams(vmem_limit_bytes=limit),
        cost_estimate=pl.CostEstimate(flops=flops, bytes_accessed=nbytes, transcendentals=0),
    )(*lead, *args)


def body(vorticity, layer_to_mode, mode_to_layer, inverse_radii, wind_curl, wet_mask):
    field = ((NL, ROWS, N), f32)
    plane = ((ROWS, N), f32)
    edge = ((NL, N), f32)
    mixing = ((NL, NL), f32)
    sines = ((PIECES, N, STEP), bf16)
    packet = ((BLOCKS, 1, 2 * LANES), f32)
    rows = ((ROWS, NL, N), f32)
    rates = pltpu.SMEM((NL,), f32)
    parts = [((TALL, NL, N), f32), ((NL * TALL, NL * TALL), f32)]
    weights = [field, ((NL, 8, ROWS, N), f32), plane]
    wave = ((NL * TALL, N), f32)

    index = (lax.axis_index("group") * lax.axis_size("tile") + lax.axis_index("tile")).astype(i32).reshape(1)
    outs = [packet, rows, edge, edge, sines, sines]
    send, force, first, last, high, low = call(
        forward_kernel, outs, (vorticity, layer_to_mode, inverse_radii, jnp.asarray(host_table())),
        [field, mixing, rates, ((4, 32, N), f32), *outs, DMA((7 + 3 * PIECES,))],
        6 * 128 * N * N, 6 << 20,
    )
    take = lax.all_to_all(send, AXES, split_axis=0, concat_axis=0, tiled=True)
    south = lax.ppermute(last, AXES, [(i, i + 1) for i in range(BLOCKS - 1)])
    north = lax.ppermute(first, AXES, [(i + 1, i) for i in range(BLOCKS - 1)])
    part, mixed = call(
        part_kernel, parts, (force, inverse_radii, mode_to_layer), [rows, rates, mixing, *parts, DMA((5,))],
        1 << 24, 1 << 20,
    )
    (give,) = call(
        scan_kernel, [packet], (inverse_radii, take, part, south, north), [rates, packet, packet, DMA((2,))],
        1 << 22, 1 << 18, index,
    )
    amplitude = lax.all_to_all(give, AXES, split_axis=0, concat_axis=0, tiled=True)
    base, coef, drag = call(
        weight_kernel, weights, (vorticity, wind_curl, wet_mask, south, north, give),
        [field, plane, ((ROWS, N), i32), edge, edge, *weights, DMA((11,))],
        1 << 24, 5 << 20,
    )
    return tuple(
        call(
            backward_kernel, [field, field],
            (inverse_radii, amplitude, part, mixed, high, low, base, coef, drag),
            [rates, packet, *parts, sines, sines, *weights, wave, wave, field, field, DMA((14,))],
            6 * 160 * N * N, 10 << 20, index,
        )
    )


def solution(mesh):
    rows = P(None, AXES, None)
    return jax.shard_map(
        body,
        mesh=mesh,
        in_specs=(rows, P(), P(), P(), P(AXES, None), P(AXES, None)),
        out_specs=(rows, rows),
        check_vma=False,
    )
```

```python
import math

import jax
import jax.numpy as jnp
import numpy as np
from jax import lax
from jax.experimental import pallas as pl
from jax.experimental.pallas import tpu as pltpu
from jax.sharding import PartitionSpec as P

time_step = 0.5
beta_plane = 1.0
bottom_drag = 0.2

N = 1024
NL = 16
ROWS = 8
TALL = ROWS + 2
BLOCKS = 128
LANES = 128
STEP = 256
PIECES = N // STEP
AXES = ("group", "tile")
HIGHEST = lax.Precision.HIGHEST
SMEM = pl.BlockSpec(memory_space=pltpu.SMEM)
VMEM = pl.BlockSpec(memory_space=pltpu.VMEM)
ANY = pl.BlockSpec(memory_space=pl.ANY)
DMA = pltpu.SemaphoreType.DMA
f32, bf16, i32 = jnp.float32, jnp.bfloat16, jnp.int32


def host_table():
    k = np.arange(1, N + 1)
    turn = 2 * (N + 1)
    angle_a = np.pi * ((32 * np.arange(32)[:, None] * k[None, :]) % turn) / (N + 1)
    angle_b = np.pi * ((np.arange(1, 33)[:, None] * k[None, :]) % turn) / (N + 1)
    scale = math.sqrt(2.0 / (N + 1))
    table = [np.sin(angle_a), np.cos(angle_a), scale * np.sin(angle_b), scale * np.cos(angle_b)]
    return np.stack(table).astype(np.float32)


def iota(shape, dim):
    return lax.broadcasted_iota(jnp.int32, shape, dim)


def dot(left, right, precision=None):
    return lax.dot_general(
        left, right, (((1,), (0,)), ((), ())), precision=precision, preferred_element_type=jnp.float32
    )


def halves(value):
    high = value.astype(jnp.bfloat16)
    low = (value - high.astype(jnp.float32)).astype(jnp.bfloat16)
    return high, low


def split_dot(left, right):
    count = left[0].shape[0]
    both = dot(jnp.concatenate(left, 0), right[0])
    return both[:count] + both[count:] + dot(left[0], right[1])


def fetch(pairs, sems, first=0):
    copies = [pltpu.make_async_copy(src, dst, sems.at[first + i]) for i, (src, dst) in enumerate(pairs)]
    for copy in copies:
        copy.start()
    return copies


def wait(copies):
    for copy in copies:
        copy.wait()


def eigen_values(first, width):
    wave = (iota((1, width), 1) + (first + 1)).astype(jnp.float32)
    angle = wave * (math.pi / (2 * (N + 1)))
    square = angle * angle
    series = jnp.full_like(square, 1.0 / math.factorial(15))
    for order in (13, 11, 9, 7, 5, 3, 1):
        series = 1.0 / math.factorial(order) - square * series
    sine = angle * series
    return 4.0 * sine * sine


def radii_column(radii_ref, shape):
    sub = iota(shape, 0)
    column = jnp.zeros(shape, jnp.float32)
    for m in range(NL):
        column = jnp.where(sub == m, radii_ref[m], column)
    return column


def decay_of(shift):
    half = 0.5 * jnp.sqrt(shift)
    root = jnp.sqrt(1.0 + 0.25 * shift)
    grow = half + root
    return 1.0 / (grow * grow), 1.0 / (4.0 * half * root)


def mode_decay(radii_ref):
    return decay_of(eigen_values(0, N) + radii_column(radii_ref, (NL, N)))


def forward_kernel(
    vortex_hbm, mix_hbm, radii_hbm, table_hbm,
    send_hbm, force_hbm, high_hbm, low_hbm,
    vortex_ref, mix_ref, radii_ref, table_ref,
    send_ref, force_ref, high_ref, low_ref, sems,
):
    copies = fetch(
        [(mix_hbm, mix_ref), (radii_hbm, radii_ref), (vortex_hbm, vortex_ref), (table_hbm, table_ref)], sems
    )
    rows = NL * ROWS
    spread = (iota((NL, rows), 1) // ROWS == iota((NL, rows), 0)).astype(jnp.float32)
    wait(copies[:2])
    rho, weight = mode_decay(radii_ref)
    wide = dot(mix_ref[...], spread, HIGHEST)
    mix = jnp.concatenate([wide] * ROWS, 0)
    mix = jnp.where(iota((rows, rows), 0) // NL == iota((rows, rows), 1) % ROWS, mix, 0.0)
    wait(copies[2:3])
    written = []
    for c in range(N // LANES):
        part = slice(c * LANES, (c + 1) * LANES)
        send_ref[c * NL : (c + 1) * NL, 0, 2 * LANES : 3 * LANES] = vortex_ref[:, ROWS - 1, part]
        send_ref[c * NL : (c + 1) * NL, 0, 3 * LANES :] = vortex_ref[:, 0, part]
    modal = split_dot(halves(mix), halves(vortex_ref[...].reshape(rows, N)))
    split = halves(modal)
    wait(copies[3:])
    for n in range(PIECES):
        cols = slice(n * STEP, (n + 1) * STEP)
        for a in range(32):
            block = table_ref[0, a : a + 1, cols] * table_ref[3, :, cols]
            block += table_ref[1, a : a + 1, cols] * table_ref[2, :, cols]
            high, low = halves(block)
            high_ref[n, 32 * a : 32 * a + 32] = high
            low_ref[n, 32 * a : 32 * a + 32] = low
        written += fetch([(high_ref.at[n], high_hbm.at[n]), (low_ref.at[n], low_hbm.at[n])], sems, 4 + 3 * n)
        spectrum = split_dot(split, (high_ref[n], low_ref[n]))
        right = jnp.zeros((NL, STEP), jnp.float32)
        left = jnp.zeros((NL, STEP), jnp.float32)
        force = []
        for y in range(ROWS):
            force.append(-weight[:, cols] * spectrum[y * NL : (y + 1) * NL])
            force_ref[y, :, cols] = force[y]
            right = rho[:, cols] * right + force[y]
        for y in reversed(range(ROWS)):
            left = rho[:, cols] * left + force[y]
        for c in range(STEP // LANES):
            dest = n * (STEP // LANES) + c
            part = slice(c * LANES, (c + 1) * LANES)
            send_ref[dest * NL : (dest + 1) * NL, 0, :LANES] = right[:, part]
            send_ref[dest * NL : (dest + 1) * NL, 0, LANES : 2 * LANES] = left[:, part]
        dests = pl.ds(n * (STEP // LANES) * NL, STEP // LANES * NL)
        written += fetch([(send_ref.at[dests], send_hbm.at[dests])], sems, 6 + 3 * n)
    written += fetch([(force_ref, force_hbm)], sems, 4 + 3 * PIECES)
    wait(written)


def shift_rows(value, step):
    blank = jnp.zeros((abs(step), value.shape[1]), value.dtype)
    if step > 0:
        return jnp.concatenate([blank, value[:-step]], 0)
    return jnp.concatenate([value[-step:], blank], 0)


def scan_kernel(
    index_ref, take_ref, radii_hbm, after_hbm, give_hbm, radii_ref, give_ref, sems
):
    del after_hbm
    wait(fetch([(radii_hbm, radii_ref)], sems))
    me = index_ref[0]
    rho, _ = decay_of(eigen_values(me // NL * LANES, LANES) + radii_ref[me % NL])
    rho2 = rho * rho
    rho4 = rho2 * rho2
    place = iota((BLOCKS, LANES), 0)
    rates = [rho4 * rho4]
    while 2 ** len(rates) <= BLOCKS:
        rates.append(rates[-1] * rates[-1])
    power = jnp.ones((BLOCKS, LANES), jnp.float32)
    reverse = power
    for bit, rate in enumerate(rates[:-1]):
        odd = (place >> bit) % 2 == 1
        power = power * jnp.where(odd, rate, 1.0)
        reverse = reverse * jnp.where(odd, 1.0, rate)
    right = take_ref[:, 0, :LANES]
    left = take_ref[:, 0, LANES : 2 * LANES]
    for bit, rate in enumerate(rates[:-1]):
        right = right + rate * shift_rows(right, 1 << bit)
        left = left + rate * shift_rows(left, -1 << bit)
    below = rho * left[:1]
    above = rho * right[BLOCKS - 1 :]
    far = rates[-1] * rho
    scale = 1.0 / (1.0 - far * far)
    alpha = -(below - far * above) * scale
    beta = -(above - far * below) * scale
    give_ref[:, 0, :LANES] = shift_rows(right, 1) + alpha * power
    give_ref[:, 0, LANES : 2 * LANES] = shift_rows(left, -1) + beta * reverse
    give_ref[:, 0, 2 * LANES : 3 * LANES] = shift_rows(take_ref[:, 0, 2 * LANES : 3 * LANES], 1)
    give_ref[:, 0, 3 * LANES :] = shift_rows(take_ref[:, 0, 3 * LANES :], -1)
    wait(fetch([(give_ref, give_hbm)], sems))


def part_kernel(
    force_hbm, radii_hbm, mix_hbm, part_hbm, mixed_hbm, force_ref, radii_ref, mix_ref, part_ref, mixed_ref, sems
):
    copies = fetch([(radii_hbm, radii_ref), (mix_hbm, mix_ref), (force_hbm, force_ref)], sems)
    wait(copies[:2])
    tall = NL * TALL
    row = iota((tall, NL), 0)
    layer = jnp.where(row < NL * ROWS, row // ROWS, row % NL)
    pick = (layer == iota((tall, NL), 1)).astype(jnp.float32)
    wide = (iota((NL, tall), 1) % NL == iota((NL, tall), 0)).astype(jnp.float32)
    mixed = dot(dot(pick, mix_ref[...], HIGHEST), wide, HIGHEST)
    row = iota((tall, tall), 0)
    place = jnp.where(row < NL * ROWS, row % ROWS + 1, jnp.where(row < NL * (ROWS + 1), 0, ROWS + 1))
    mixed_ref[...] = jnp.where(iota((tall, tall), 1) // NL == place, mixed, 0.0)
    written = fetch([(mixed_ref, mixed_hbm)], sems, 3)
    rho, _ = mode_decay(radii_ref)
    wait(copies[2:])
    right = jnp.zeros((NL, N), jnp.float32)
    for y in range(ROWS):
        right = rho * right + force_ref[y]
        part_ref[y + 1] = right
    part_ref[ROWS + 1] = rho * right
    left = jnp.zeros((NL, N), jnp.float32)
    for y in reversed(range(ROWS)):
        part_ref[y + 1] += left
        left = rho * (left + force_ref[y])
    part_ref[0] = left
    wait(written + fetch([(part_ref, part_hbm)], sems, 4))


def roll_lanes(value, step):
    width = value.shape[1]
    lane = iota(value.shape, 1)
    rolled = pltpu.roll(value, step % width, 1)
    return jnp.where(lane == (0 if step > 0 else width - 1), 0.0, rolled)


def roll_sub(value, edge, step):
    height = value.shape[0]
    sub = iota(value.shape, 0)
    rolled = pltpu.roll(value, step % height, 0)
    return jnp.where(sub == (0 if step > 0 else height - 1), edge, rolled)


def weight_kernel(
    vortex_hbm, wind_hbm, wet_hbm, after_hbm, coef_hbm, vortex_ref, wind_ref, wet_ref, coef_ref, sems
):
    del after_hbm
    wait(
        fetch(
            [(wet_hbm, wet_ref), (wind_hbm, wind_ref), (vortex_hbm, vortex_ref)], sems
        )
    )
    keep = time_step * wet_ref[...].astype(jnp.float32)
    twelfth = keep * (1.0 / 12.0)
    written = []
    for layer in range(NL):
        mid = vortex_ref[layer]
        north = roll_sub(mid, 0.0, -1)
        south = roll_sub(mid, 0.0, 1)
        east = roll_lanes(mid, -1)
        west = roll_lanes(mid, 1)
        north_east = roll_lanes(north, -1)
        north_west = roll_lanes(north, 1)
        south_east = roll_lanes(south, -1)
        south_west = roll_lanes(south, 1)
        along = north - south
        across = east - west
        c_east = -twelfth * (along + (north_east - south_east)) - keep * (0.5 * beta_plane)
        c_west = twelfth * (along + (north_west - south_west)) + keep * (0.5 * beta_plane)
        c_north = twelfth * (across + (north_east - north_west))
        c_south = -twelfth * (across + (south_east - south_west))
        if layer == NL - 1:
            drag = keep * bottom_drag
            c_east = c_east - drag
            c_west = c_west - drag
            c_north = c_north - drag
            c_south = c_south - drag
            coef_ref[NL, 0] = 4.0 * drag
            coef_ref[NL, 1] = twelfth
        coef_ref[layer, 0] = c_north
        coef_ref[layer, 1] = c_south
        coef_ref[layer, 2] = roll_lanes(c_east, 1)
        coef_ref[layer, 3] = roll_lanes(-twelfth * (north - east), 1)
        coef_ref[layer, 4] = roll_lanes(twelfth * (south - east), 1)
        coef_ref[layer, 5] = roll_lanes(c_west, -1)
        coef_ref[layer, 6] = roll_lanes(twelfth * (north - west), -1)
        coef_ref[layer, 7] = roll_lanes(-twelfth * (south - west), -1)
        coef_ref[layer, 8] = mid + keep * wind_ref[...] if layer == 0 else mid
        if layer % 4 == 3:
            some = pl.ds(layer - 3, 4 if layer < NL - 1 else 5)
            written += fetch([(coef_ref.at[some], coef_hbm.at[some])], sems, 3 + layer // 4)
    wait(written)


def backward_kernel(
    index_ref, take_ref, part_ref, mixed_ref, radii_hbm, high_hbm, low_hbm, coef_hbm, vortex_hbm, stream_hbm,
    radii_ref, high_ref, low_ref, coef_ref, psi_ref, south_ref, north_ref, wave_ref, vortex_ref, stream_ref, sems,
):
    copies = fetch(
        [(radii_hbm, radii_ref), (high_hbm, high_ref), (low_hbm, low_ref), (coef_hbm, coef_ref)], sems
    )
    out = len(copies)
    copies[0].wait()
    rho, _ = mode_decay(radii_ref)
    for c in range(N // LANES):
        cols = slice(c * LANES, (c + 1) * LANES)
        up = take_ref[c * NL : (c + 1) * NL, 0, :LANES]
        down = take_ref[c * NL : (c + 1) * NL, 0, LANES : 2 * LANES]
        south_ref[:, cols] = take_ref[c * NL : (c + 1) * NL, 0, 2 * LANES : 3 * LANES]
        north_ref[:, cols] = take_ref[c * NL : (c + 1) * NL, 0, 3 * LANES :]
        near = rho[:, cols]
        ups, downs = [up], [down]
        for _ in range(ROWS + 1):
            ups.append(ups[-1] * near)
            downs.append(downs[-1] * near)
        for i in range(TALL):
            psi_ref[i * NL : (i + 1) * NL, cols] = part_ref[i, :, cols] + ups[i] + downs[ROWS + 1 - i]
    split = halves(split_dot(halves(mixed_ref[...]), halves(psi_ref[...])))
    wait(copies[1:3])
    for n in range(PIECES):
        wave_ref[:, n * STEP : (n + 1) * STEP] = split_dot(split, (high_ref[n], low_ref[n]))
    inside_low = jnp.where(index_ref[0] > 0, 1.0, 0.0)
    inside_high = jnp.where(index_ref[0] < BLOCKS - 1, 1.0, 0.0)
    body = NL * ROWS
    for layer in range(NL):
        stream_ref[layer] = wave_ref[layer * ROWS : (layer + 1) * ROWS]
    written = fetch([(stream_ref, stream_hbm)], sems, out)
    wait(copies[3:])
    twelfth = coef_ref[NL, 1]
    for y, edge_ref, beyond, sign in (
        (0, south_ref, inside_low * wave_ref[body : body + NL], 1.0),
        (ROWS - 1, north_ref, inside_high * wave_ref[body + NL :], -1.0),
    ):
        here = stream_ref[:, y]
        edge = edge_ref[...]
        east, west = roll_lanes(edge, -1), roll_lanes(edge, 1)
        more = roll_lanes(here, -1) * (edge + east) - roll_lanes(here, 1) * (edge + west)
        more += edge * (roll_lanes(beyond, -1) - roll_lanes(beyond, 1)) - beyond * (east - west)
        coef_ref[:NL, 8, y] += sign * twelfth[y : y + 1] * more
    for layer in range(NL):
        mid = wave_ref[layer * ROWS : (layer + 1) * ROWS]
        north = roll_sub(mid, inside_high * wave_ref[body + NL + layer : body + NL + layer + 1], -1)
        south = roll_sub(mid, inside_low * wave_ref[body + layer : body + layer + 1], 1)
        total = coef_ref[layer, 8] + coef_ref[layer, 0] * north + coef_ref[layer, 1] * south
        if layer == NL - 1:
            total = total + coef_ref[NL, 0] * mid
        from_east = coef_ref[layer, 2] * mid + coef_ref[layer, 3] * north + coef_ref[layer, 4] * south
        from_west = coef_ref[layer, 5] * mid + coef_ref[layer, 6] * north + coef_ref[layer, 7] * south
        vortex_ref[layer] = total + pltpu.roll(from_east, N - 1, 1) + pltpu.roll(from_west, 1, 1)
        if layer % 4 == 3:
            some = pl.ds(layer - 3, 4)
            written += fetch([(vortex_ref.at[some], vortex_hbm.at[some])], sems, out + 1 + layer // 4)
    wait(written)


def call(kernel, outs, args, scratch, flops, nbytes, scalars=(), near=(), limit=60 * 1024 * 1024):
    def room(kind):
        return pltpu.VMEM(*kind) if isinstance(kind, tuple) else kind

    return pl.pallas_call(
        kernel,
        out_shape=[jax.ShapeDtypeStruct(s, d) for s, d in outs],
        in_specs=[SMEM] * len(scalars) + [VMEM] * len(near) + [ANY] * len(args),
        out_specs=[ANY] * len(outs),
        scratch_shapes=[room(kind) for kind in scratch],
        compiler_params=pltpu.CompilerParams(vmem_limit_bytes=limit),
        cost_estimate=pl.CostEstimate(flops=flops, bytes_accessed=nbytes, transcendentals=0),
    )(*scalars, *near, *args)


def body(vorticity, layer_to_mode, mode_to_layer, inverse_radii, wind_curl, wet_mask):
    field = ((NL, ROWS, N), f32)
    plane = ((ROWS, N), f32)
    edge = ((NL, N), f32)
    mixing = ((NL, NL), f32)
    sines = ((PIECES, N, STEP), bf16)
    packet = ((BLOCKS, 1, 4 * LANES), f32)
    rows = ((ROWS, NL, N), f32)
    rates = pltpu.SMEM((NL,), f32)
    parts = [((TALL, NL, N), f32), ((NL * TALL, NL * TALL), f32)]
    weights = ((NL + 1, 9, ROWS, N), f32)
    wave = ((NL * TALL, N), f32)

    index = (lax.axis_index("group") * lax.axis_size("tile") + lax.axis_index("tile")).astype(i32).reshape(1)
    outs = [packet, rows, sines, sines]
    send, force, high, low = call(
        forward_kernel, outs, (vorticity, layer_to_mode, inverse_radii, jnp.asarray(host_table())),
        [field, mixing, rates, ((4, 32, N), f32), *outs, DMA((5 + 3 * PIECES,))],
        6 * 128 * N * N, 6 << 20,
    )
    take = lax.all_to_all(send, AXES, split_axis=0, concat_axis=0, tiled=True)
    part, mixed = call(
        part_kernel, parts, (force, inverse_radii, mode_to_layer), [rows, rates, mixing, *parts, DMA((5,))],
        1 << 24, 1 << 20,
    )
    (give,) = call(
        scan_kernel, [packet], (inverse_radii, part), [rates, packet, DMA((1,))],
        1 << 22, 1 << 18, [index], [take], limit=54500 << 10,
    )
    amplitude = lax.all_to_all(give, AXES, split_axis=0, concat_axis=0, tiled=True)
    (coef,) = call(
        weight_kernel, [weights], (vorticity, wind_curl, wet_mask, give),
        [field, plane, ((ROWS, N), i32), weights, DMA((7,))],
        1 << 24, 5 << 20,
    )
    return tuple(
        call(
            backward_kernel, [field, field],
            (inverse_radii, high, low, coef),
            [rates, sines, sines, weights, wave, edge, edge, wave, field, field, DMA((9,))],
            6 * 160 * N * N, 10 << 20, [index], [amplitude, part, mixed], limit=53500 << 10,
        )
    )


def solution(mesh):
    rows = P(None, AXES, None)
    return jax.shard_map(
        body,
        mesh=mesh,
        in_specs=(rows, P(), P(), P(), P(AXES, None), P(AXES, None)),
        out_specs=(rows, rows),
        check_vma=False,
    )
```

```python
import math

import jax
import jax.numpy as jnp
import numpy as np
from jax import lax
from jax.experimental import pallas as pl
from jax.experimental.pallas import tpu as pltpu
from jax.sharding import PartitionSpec as P

time_step = 0.5
beta_plane = 1.0
bottom_drag = 0.2

N = 1024
NL = 16
ROWS = 8
TALL = ROWS + 2
BLOCKS = 128
LANES = 128
HALF = N // 2
STEP = 256
PIECES = N // STEP
AXES = ("group", "tile")
HIGHEST = lax.Precision.HIGHEST
SMEM = pl.BlockSpec(memory_space=pltpu.SMEM)
VMEM = pl.BlockSpec(memory_space=pltpu.VMEM)
ANY = pl.BlockSpec(memory_space=pl.ANY)
DMA = pltpu.SemaphoreType.DMA
f32, bf16, i32 = jnp.float32, jnp.bfloat16, jnp.int32


def host_table():
    k = np.arange(1, N + 1)
    sine = math.sqrt(2.0 / (N + 1)) * np.sin(np.pi * ((k[:, None] * k[None, :]) % (2 * (N + 1))) / (N + 1))
    table = np.stack([sine[:HALF, 0::2], sine[:HALF, 1::2]])
    high = table.astype(jnp.bfloat16)
    low = (table - high.astype(np.float64)).astype(jnp.bfloat16)
    return np.stack([high, low], 1)


def iota(shape, dim):
    return lax.broadcasted_iota(jnp.int32, shape, dim)


def dot(left, right, precision=None, across=0):
    return lax.dot_general(
        left, right, (((1,), (across,)), ((), ())), precision=precision, preferred_element_type=jnp.float32
    )


def halves(value):
    high = value.astype(jnp.bfloat16)
    low = (value - high.astype(jnp.float32)).astype(jnp.bfloat16)
    return high, low


def split_dot(left, right, across=0):
    count = left[0].shape[0]
    both = dot(jnp.concatenate(left, 0), right[0], None, across)
    return both[:count] + both[count:] + dot(left[0], right[1], None, across)


def mirrored(value):
    flip = (iota((STEP, STEP), 0) + iota((STEP, STEP), 1) == STEP - 1).astype(jnp.bfloat16)
    count, width = value.shape
    parts = jnp.concatenate(halves(value), 0)
    blocks = [dot(parts[:, i : i + STEP], flip) for i in range(0, width, STEP)]
    return jnp.concatenate([block[:count] + block[count:] for block in reversed(blocks)], 1)


def fetch(pairs, sems, first=0):
    copies = [pltpu.make_async_copy(src, dst, sems.at[first + i]) for i, (src, dst) in enumerate(pairs)]
    for copy in copies:
        copy.start()
    return copies


def wait(copies):
    for copy in copies:
        copy.wait()


def eigen_values(first, width):
    column = iota((1, width), 1) + first
    wave = jnp.where(column < HALF, 2 * column + 1, 2 * column + 2 - N).astype(jnp.float32)
    angle = wave * (math.pi / (2 * (N + 1)))
    square = angle * angle
    series = jnp.full_like(square, 1.0 / math.factorial(15))
    for order in (13, 11, 9, 7, 5, 3, 1):
        series = 1.0 / math.factorial(order) - square * series
    sine = angle * series
    return 4.0 * sine * sine


def radii_column(radii_ref, shape):
    sub = iota(shape, 0)
    column = jnp.zeros(shape, jnp.float32)
    for m in range(NL):
        column = jnp.where(sub == m, radii_ref[m], column)
    return column


def decay_of(shift):
    half = 0.5 * jnp.sqrt(shift)
    root = jnp.sqrt(1.0 + 0.25 * shift)
    grow = half + root
    return 1.0 / (grow * grow), 1.0 / (4.0 * half * root)


def mode_decay(radii_ref):
    return decay_of(eigen_values(0, N) + radii_column(radii_ref, (NL, N)))


def forward_kernel(
    vortex_hbm, mix_hbm, radii_hbm, table_hbm,
    send_hbm, force_hbm,
    vortex_ref, mix_ref, radii_ref, table_ref, send_ref, force_ref, sems,
):
    copies = fetch(
        [
            (mix_hbm, mix_ref), (radii_hbm, radii_ref), (vortex_hbm, vortex_ref),
            (table_hbm.at[0], table_ref.at[0]), (table_hbm.at[1], table_ref.at[1]),
        ],
        sems,
    )
    rows = NL * ROWS
    spread = (iota((NL, rows), 1) // ROWS == iota((NL, rows), 0)).astype(jnp.float32)
    wait(copies[:2])
    rho, weight = mode_decay(radii_ref)
    wide = dot(mix_ref[...], spread, HIGHEST)
    mix = jnp.concatenate([wide] * ROWS, 0)
    mix = jnp.where(iota((rows, rows), 0) // NL == iota((rows, rows), 1) % ROWS, mix, 0.0)
    wait(copies[2:3])
    written = []
    for c in range(N // LANES):
        part = slice(c * LANES, (c + 1) * LANES)
        send_ref[c * NL : (c + 1) * NL, 0, 2 * LANES : 3 * LANES] = vortex_ref[:, ROWS - 1, part]
        send_ref[c * NL : (c + 1) * NL, 0, 3 * LANES :] = vortex_ref[:, 0, part]
    modal = split_dot(halves(mix), halves(vortex_ref[...].reshape(rows, N)))
    mirror = mirrored(modal[:, HALF:])
    folded = [halves(modal[:, :HALF] + mirror), halves(modal[:, :HALF] - mirror)]
    for n in range(PIECES):
        cols = slice(n * STEP, (n + 1) * STEP)
        odd, start = divmod(n * STEP, HALF)
        if start == 0:
            copies[3 + odd].wait()
        some = slice(start, start + STEP)
        spectrum = split_dot(folded[odd], (table_ref[odd, 0, :, some], table_ref[odd, 1, :, some]))
        right = jnp.zeros((NL, STEP), jnp.float32)
        left = jnp.zeros((NL, STEP), jnp.float32)
        force = []
        for y in range(ROWS):
            force.append(-weight[:, cols] * spectrum[y * NL : (y + 1) * NL])
            force_ref[y, :, cols] = force[y]
            right = rho[:, cols] * right + force[y]
        for y in reversed(range(ROWS)):
            left = rho[:, cols] * left + force[y]
        for c in range(STEP // LANES):
            dest = n * (STEP // LANES) + c
            part = slice(c * LANES, (c + 1) * LANES)
            send_ref[dest * NL : (dest + 1) * NL, 0, :LANES] = right[:, part]
            send_ref[dest * NL : (dest + 1) * NL, 0, LANES : 2 * LANES] = left[:, part]
        dests = pl.ds(n * (STEP // LANES) * NL, STEP // LANES * NL)
        written += fetch([(send_ref.at[dests], send_hbm.at[dests])], sems, 5 + n)
    written += fetch([(force_ref, force_hbm)], sems, 5 + PIECES)
    wait(written)


def shift_rows(value, step):
    blank = jnp.zeros((abs(step), value.shape[1]), value.dtype)
    if step > 0:
        return jnp.concatenate([blank, value[:-step]], 0)
    return jnp.concatenate([value[-step:], blank], 0)


def scan_kernel(take_ref, ends_ref, give_hbm, give_ref, sems):
    rates = [ends_ref[2 * BLOCKS + bit : 2 * BLOCKS + bit + 1] for bit in range(8)]
    rho = ends_ref[2 * BLOCKS + 8 : 2 * BLOCKS + 9]
    right = take_ref[:, 0, :LANES]
    left = take_ref[:, 0, LANES : 2 * LANES]
    for bit, rate in enumerate(rates[:-1]):
        right = right + rate * shift_rows(right, 1 << bit)
        left = left + rate * shift_rows(left, -1 << bit)
    below = rho * left[:1]
    above = rho * right[BLOCKS - 1 :]
    far = rates[-1] * rho
    scale = 1.0 / (1.0 - far * far)
    alpha = -(below - far * above) * scale
    beta = -(above - far * below) * scale
    give_ref[:, 0, :LANES] = shift_rows(right, 1) + alpha * ends_ref[:BLOCKS]
    give_ref[:, 0, LANES : 2 * LANES] = shift_rows(left, -1) + beta * ends_ref[BLOCKS : 2 * BLOCKS]
    give_ref[:, 0, 2 * LANES : 3 * LANES] = shift_rows(take_ref[:, 0, 2 * LANES : 3 * LANES], 1)
    give_ref[:, 0, 3 * LANES :] = shift_rows(take_ref[:, 0, 3 * LANES :], -1)
    wait(fetch([(give_ref, give_hbm)], sems))


def part_kernel(
    index_ref, force_hbm, radii_hbm, mix_hbm, part_hbm, mixed_hbm, ends_ref,
    force_ref, radii_ref, mix_ref, part_ref, mixed_ref, sems,
):
    copies = fetch([(radii_hbm, radii_ref), (mix_hbm, mix_ref), (force_hbm, force_ref)], sems)
    wait(copies[:2])
    me = index_ref[0]
    rho, _ = decay_of(eigen_values(me // NL * LANES, LANES) + radii_ref[me % NL])
    rate = rho
    for _ in range(3):
        rate = rate * rate
    place = iota((BLOCKS, LANES), 0)
    power = jnp.ones((BLOCKS, LANES), jnp.float32)
    reverse = power
    for bit in range(8):
        ends_ref[2 * BLOCKS + bit : 2 * BLOCKS + bit + 1] = rate
        if bit < 7:
            odd = (place >> bit) % 2 == 1
            power = power * jnp.where(odd, rate, 1.0)
            reverse = reverse * jnp.where(odd, 1.0, rate)
        rate = rate * rate
    ends_ref[2 * BLOCKS + 8 : 2 * BLOCKS + 9] = rho
    ends_ref[:BLOCKS] = power
    ends_ref[BLOCKS : 2 * BLOCKS] = reverse
    tall = NL * TALL
    row = iota((tall, NL), 0)
    layer = jnp.where(row < NL * ROWS, row // ROWS, row % NL)
    pick = (layer == iota((tall, NL), 1)).astype(jnp.float32)
    wide = (iota((NL, tall), 1) % NL == iota((NL, tall), 0)).astype(jnp.float32)
    mixed = dot(dot(pick, mix_ref[...], HIGHEST), wide, HIGHEST)
    row = iota((tall, tall), 0)
    place = jnp.where(row < NL * ROWS, row % ROWS + 1, jnp.where(row < NL * (ROWS + 1), 0, ROWS + 1))
    mixed_ref[...] = jnp.where(iota((tall, tall), 1) // NL == place, mixed, 0.0)
    written = fetch([(mixed_ref, mixed_hbm)], sems, 3)
    rho, _ = mode_decay(radii_ref)
    part_ref[TALL] = rho
    wait(copies[2:])
    right = jnp.zeros((NL, N), jnp.float32)
    for y in range(ROWS):
        right = rho * right + force_ref[y]
        part_ref[y + 1] = right
    part_ref[ROWS + 1] = rho * right
    left = jnp.zeros((NL, N), jnp.float32)
    for y in reversed(range(ROWS)):
        part_ref[y + 1] += left
        left = rho * (left + force_ref[y])
    part_ref[0] = left
    wait(written + fetch([(part_ref, part_hbm)], sems, 4))


def roll_lanes(value, step):
    width = value.shape[1]
    lane = iota(value.shape, 1)
    rolled = pltpu.roll(value, step % width, 1)
    return jnp.where(lane == (0 if step > 0 else width - 1), 0.0, rolled)


def roll_sub(value, edge, step):
    height = value.shape[0]
    sub = iota(value.shape, 0)
    rolled = pltpu.roll(value, step % height, 0)
    return jnp.where(sub == (0 if step > 0 else height - 1), edge, rolled)


def weight_kernel(
    vortex_hbm, wind_hbm, wet_hbm, after_hbm, coef_hbm, vortex_ref, wind_ref, wet_ref, coef_ref, sems
):
    del after_hbm
    wait(
        fetch(
            [(wet_hbm, wet_ref), (wind_hbm, wind_ref), (vortex_hbm, vortex_ref)], sems
        )
    )
    keep = time_step * wet_ref[...].astype(jnp.float32)
    twelfth = keep * (1.0 / 12.0)
    written = []
    for layer in range(NL):
        mid = vortex_ref[layer]
        north = roll_sub(mid, 0.0, -1)
        south = roll_sub(mid, 0.0, 1)
        east = roll_lanes(mid, -1)
        west = roll_lanes(mid, 1)
        north_east = roll_lanes(north, -1)
        north_west = roll_lanes(north, 1)
        south_east = roll_lanes(south, -1)
        south_west = roll_lanes(south, 1)
        along = north - south
        across = east - west
        c_east = -twelfth * (along + (north_east - south_east)) - keep * (0.5 * beta_plane)
        c_west = twelfth * (along + (north_west - south_west)) + keep * (0.5 * beta_plane)
        c_north = twelfth * (across + (north_east - north_west))
        c_south = -twelfth * (across + (south_east - south_west))
        if layer == NL - 1:
            drag = keep * bottom_drag
            c_east = c_east - drag
            c_west = c_west - drag
            c_north = c_north - drag
            c_south = c_south - drag
            coef_ref[NL, 0] = 4.0 * drag
            coef_ref[NL, 1] = twelfth
        coef_ref[layer, 0] = c_north
        coef_ref[layer, 1] = c_south
        coef_ref[layer, 2] = roll_lanes(c_east, 1)
        coef_ref[layer, 3] = roll_lanes(-twelfth * (north - east), 1)
        coef_ref[layer, 4] = roll_lanes(twelfth * (south - east), 1)
        coef_ref[layer, 5] = roll_lanes(c_west, -1)
        coef_ref[layer, 6] = roll_lanes(twelfth * (north - west), -1)
        coef_ref[layer, 7] = roll_lanes(-twelfth * (south - west), -1)
        coef_ref[layer, 8] = mid + keep * wind_ref[...] if layer == 0 else mid
        if layer % 4 == 3:
            some = pl.ds(layer - 3, 4 if layer < NL - 1 else 5)
            written += fetch([(coef_ref.at[some], coef_hbm.at[some])], sems, 3 + layer // 4)
    wait(written)


def backward_kernel(
    index_ref, take_ref, part_ref, mixed_ref, table_ref, coef_hbm, vortex_hbm, stream_hbm, coef_ref, psi_ref, south_ref, north_ref, wave_ref, vortex_ref, stream_ref, sems,
):
    copies = fetch([(coef_hbm.at[i], coef_ref.at[i]) for i in (NL, *range(NL))], sems)
    out = len(copies)
    for c in range(N // LANES):
        cols = slice(c * LANES, (c + 1) * LANES)
        up = take_ref[c * NL : (c + 1) * NL, 0, :LANES]
        down = take_ref[c * NL : (c + 1) * NL, 0, LANES : 2 * LANES]
        south_ref[:, cols] = take_ref[c * NL : (c + 1) * NL, 0, 2 * LANES : 3 * LANES]
        north_ref[:, cols] = take_ref[c * NL : (c + 1) * NL, 0, 3 * LANES :]
        near = part_ref[TALL, :, cols]
        ups, downs = [up], [down]
        for _ in range(ROWS + 1):
            ups.append(ups[-1] * near)
            downs.append(downs[-1] * near)
        for i in range(TALL):
            psi_ref[i * NL : (i + 1) * NL, cols] = part_ref[i, :, cols] + ups[i] + downs[ROWS + 1 - i]
    split = halves(split_dot(halves(mixed_ref[...]), halves(psi_ref[...])))
    sums = []
    for odd in range(2):
        some = tuple(part[:, odd * HALF : (odd + 1) * HALF] for part in split)
        sums.append(split_dot(some, (table_ref[odd, 0], table_ref[odd, 1]), 1))
    wave_ref[:, :HALF] = sums[0] + sums[1]
    wave_ref[:, HALF:] = mirrored(sums[0] - sums[1])
    inside_low = jnp.where(index_ref[0] > 0, 1.0, 0.0)
    inside_high = jnp.where(index_ref[0] < BLOCKS - 1, 1.0, 0.0)
    body = NL * ROWS
    for layer in range(NL):
        stream_ref[layer] = wave_ref[layer * ROWS : (layer + 1) * ROWS]
    written = fetch([(stream_ref, stream_hbm)], sems, out)
    copies[0].wait()
    twelfth = coef_ref[NL, 1]
    for y, edge_ref, beyond, sign in (
        (0, south_ref, inside_low * wave_ref[body : body + NL], 1.0),
        (ROWS - 1, north_ref, inside_high * wave_ref[body + NL :], -1.0),
    ):
        here = stream_ref[:, y]
        edge = edge_ref[...]
        east, west = roll_lanes(edge, -1), roll_lanes(edge, 1)
        more = roll_lanes(here, -1) * (edge + east) - roll_lanes(here, 1) * (edge + west)
        more += edge * (roll_lanes(beyond, -1) - roll_lanes(beyond, 1)) - beyond * (east - west)
        edge_ref[...] = sign * twelfth[y : y + 1] * more
    for layer in range(NL):
        copies[1 + layer].wait()
        mid = wave_ref[layer * ROWS : (layer + 1) * ROWS]
        north = roll_sub(mid, inside_high * wave_ref[body + NL + layer : body + NL + layer + 1], -1)
        south = roll_sub(mid, inside_low * wave_ref[body + layer : body + layer + 1], 1)
        total = coef_ref[layer, 8] + coef_ref[layer, 0] * north + coef_ref[layer, 1] * south
        if layer == NL - 1:
            total = total + coef_ref[NL, 0] * mid
        from_east = coef_ref[layer, 2] * mid + coef_ref[layer, 3] * north + coef_ref[layer, 4] * south
        from_west = coef_ref[layer, 5] * mid + coef_ref[layer, 6] * north + coef_ref[layer, 7] * south
        vortex_ref[layer] = total + pltpu.roll(from_east, N - 1, 1) + pltpu.roll(from_west, 1, 1)
        if layer % 4 == 3:
            some = slice(layer - 3, layer + 1)
            vortex_ref[some, 0] += south_ref[some]
            vortex_ref[some, ROWS - 1] += north_ref[some]
            written += fetch([(vortex_ref.at[some], vortex_hbm.at[some])], sems, out + 1 + layer // 4)
    wait(written)


def call(kernel, outs, args, scratch, flops, nbytes, scalars=(), near=(), limit=60 * 1024 * 1024, kept=0):
    def room(kind):
        return pltpu.VMEM(*kind) if isinstance(kind, tuple) else kind

    return pl.pallas_call(
        kernel,
        out_shape=[jax.ShapeDtypeStruct(s, d) for s, d in outs],
        in_specs=[SMEM] * len(scalars) + [VMEM] * len(near) + [ANY] * len(args),
        out_specs=[ANY] * (len(outs) - kept) + [VMEM] * kept,
        scratch_shapes=[room(kind) for kind in scratch],
        compiler_params=pltpu.CompilerParams(vmem_limit_bytes=limit),
        cost_estimate=pl.CostEstimate(flops=flops, bytes_accessed=nbytes, transcendentals=0),
    )(*scalars, *near, *args)


def body(vorticity, layer_to_mode, mode_to_layer, inverse_radii, wind_curl, wet_mask):
    field = ((NL, ROWS, N), f32)
    plane = ((ROWS, N), f32)
    edge = ((NL, N), f32)
    mixing = ((NL, NL), f32)
    sines = ((2, 2, HALF, HALF), bf16)
    packet = ((BLOCKS, 1, 4 * LANES), f32)
    rows = ((ROWS, NL, N), f32)
    rates = pltpu.SMEM((NL,), f32)
    parts = [((TALL + 1, NL, N), f32), ((NL * TALL, NL * TALL), f32)]
    ends = ((2 * BLOCKS + 16, LANES), f32)
    weights = ((NL + 1, 9, ROWS, N), f32)
    wave = ((NL * TALL, N), f32)

    index = (lax.axis_index("group") * lax.axis_size("tile") + lax.axis_index("tile")).astype(i32).reshape(1)
    outs = [packet, rows]
    table = jnp.asarray(host_table())
    send, force = call(
        forward_kernel, outs, (vorticity, layer_to_mode, inverse_radii, table),
        [field, mixing, rates, sines, *outs, DMA((6 + PIECES,))],
        6 * 128 * N * N, 6 << 20,
    )
    take = lax.all_to_all(send, AXES, split_axis=0, concat_axis=0, tiled=True)
    part, mixed, ends = call(
        part_kernel, parts + [ends], (force, inverse_radii, mode_to_layer), [rows, rates, mixing, *parts, DMA((5,))],
        1 << 24, 1 << 20, [index], limit=50000 << 10, kept=1,
    )
    (give,) = call(
        scan_kernel, [packet], (), [packet, DMA((1,))], 1 << 22, 1 << 18, (), [take, ends], limit=54500 << 10,
    )
    amplitude = lax.all_to_all(give, AXES, split_axis=0, concat_axis=0, tiled=True)
    (coef,) = call(
        weight_kernel, [weights], (vorticity, wind_curl, wet_mask, give),
        [field, plane, ((ROWS, N), i32), weights, DMA((7,))],
        1 << 24, 5 << 20,
    )
    return tuple(
        call(
            backward_kernel, [field, field],
            (coef,),
            [weights, wave, edge, edge, wave, field, field, DMA((NL + 6,))],
            6 * 160 * N * N, 10 << 20, [index], [amplitude, part, mixed, table], limit=51500 << 10,
        )
    )


def solution(mesh):
    rows = P(None, AXES, None)
    return jax.shard_map(
        body,
        mesh=mesh,
        in_specs=(rows, P(), P(), P(), P(AXES, None), P(AXES, None)),
        out_specs=(rows, rows),
        check_vma=False,
    )
```

```python
import math

import jax
import jax.numpy as jnp
import numpy as np
from jax import lax
from jax.experimental import pallas as pl
from jax.experimental.pallas import tpu as pltpu
from jax.sharding import PartitionSpec as P

time_step = 0.5
beta_plane = 1.0
bottom_drag = 0.2

N = 1024
NL = 16
ROWS = 8
TALL = ROWS + 2
BLOCKS = 128
LANES = 128
HALF = N // 2
STEP = 256
PIECES = N // STEP
AXES = ("group", "tile")
HIGHEST = lax.Precision.HIGHEST
SMEM = pl.BlockSpec(memory_space=pltpu.SMEM)
VMEM = pl.BlockSpec(memory_space=pltpu.VMEM)
ANY = pl.BlockSpec(memory_space=pl.ANY)
DMA = pltpu.SemaphoreType.DMA
f32, bf16, i32 = jnp.float32, jnp.bfloat16, jnp.int32


def host_table():
    k = np.arange(1, N + 1)
    sine = math.sqrt(2.0 / (N + 1)) * np.sin(np.pi * ((k[:, None] * k[None, :]) % (2 * (N + 1))) / (N + 1))
    table = np.stack([sine[:HALF, 0::2], sine[:HALF, 1::2]])
    high = table.astype(jnp.bfloat16)
    low = (table - high.astype(np.float64)).astype(jnp.bfloat16)
    return np.stack([high, low], 1)


def iota(shape, dim):
    return lax.broadcasted_iota(jnp.int32, shape, dim)


def dot(left, right, precision=None, across=0):
    return lax.dot_general(
        left, right, (((1,), (across,)), ((), ())), precision=precision, preferred_element_type=jnp.float32
    )


def halves(value):
    high = value.astype(jnp.bfloat16)
    low = (value - high.astype(jnp.float32)).astype(jnp.bfloat16)
    return high, low


def split_dot(left, right, across=0):
    count = left[0].shape[0]
    both = dot(jnp.concatenate(left, 0), right[0], None, across)
    return both[:count] + both[count:] + dot(left[0], right[1], None, across)


def mirrored(value):
    flip = (iota((STEP, STEP), 0) + iota((STEP, STEP), 1) == STEP - 1).astype(jnp.bfloat16)
    count, width = value.shape
    parts = jnp.concatenate(halves(value), 0)
    blocks = [dot(parts[:, i : i + STEP], flip) for i in range(0, width, STEP)]
    return jnp.concatenate([block[:count] + block[count:] for block in reversed(blocks)], 1)


def fetch(pairs, sems, first=0):
    copies = [pltpu.make_async_copy(src, dst, sems.at[first + i]) for i, (src, dst) in enumerate(pairs)]
    for copy in copies:
        copy.start()
    return copies


def wait(copies):
    for copy in copies:
        copy.wait()


def eigen_values(first, width):
    column = iota((1, width), 1) + first
    wave = jnp.where(column < HALF, 2 * column + 1, 2 * column + 2 - N).astype(jnp.float32)
    angle = wave * (math.pi / (2 * (N + 1)))
    square = angle * angle
    series = jnp.full_like(square, 1.0 / math.factorial(15))
    for order in (13, 11, 9, 7, 5, 3, 1):
        series = 1.0 / math.factorial(order) - square * series
    sine = angle * series
    return 4.0 * sine * sine


def radii_column(radii_ref, shape):
    sub = iota(shape, 0)
    column = jnp.zeros(shape, jnp.float32)
    for m in range(NL):
        column = jnp.where(sub == m, radii_ref[m], column)
    return column


def decay_of(shift):
    half = 0.5 * jnp.sqrt(shift)
    root = jnp.sqrt(1.0 + 0.25 * shift)
    grow = half + root
    return 1.0 / (grow * grow), 1.0 / (4.0 * half * root)


def mode_decay(radii_ref):
    return decay_of(eigen_values(0, N) + radii_column(radii_ref, (NL, N)))


def forward_kernel(
    vortex_hbm, mix_hbm, back_hbm, radii_hbm, table_hbm,
    send_hbm, carry_hbm,
    vortex_ref, mix_ref, back_ref, radii_ref, table_ref, send_ref, force_ref, sems,
):
    copies = fetch([(mix_hbm, mix_ref), (radii_hbm, radii_ref)], sems)
    layers = [pl.ds(i, 4) for i in range(0, NL, 4)]
    loads = fetch([(vortex_hbm.at[some], vortex_ref.at[some]) for some in layers], sems, 2)
    copies += fetch([(back_hbm, back_ref)], sems, 6)
    places = [(odd, low, pl.ds(i, STEP)) for odd in range(2) for low in range(2) for i in range(0, HALF, STEP)]
    waves = fetch([(table_hbm.at[place], table_ref.at[place]) for place in places], sems, 7)
    rows = NL * ROWS
    spread = (iota((NL, rows), 1) // ROWS == iota((NL, rows), 0)).astype(jnp.float32)
    wait(copies[:2])
    rho, weight = mode_decay(radii_ref)
    force_ref[2 * ROWS : 2 * ROWS + 2] = rho.reshape(2, ROWS, N)
    wide = dot(mix_ref[...], spread, HIGHEST)
    mix = jnp.concatenate([wide] * ROWS, 0)
    mix = jnp.where(iota((rows, rows), 0) // NL == iota((rows, rows), 1) % ROWS, mix, 0.0)
    wait(loads)
    written = []
    high, low = halves(mix)
    mix = jnp.concatenate([jnp.concatenate([high, high], 1), jnp.concatenate([low, jnp.zeros_like(low)], 1)], 0)
    modal = dot(mix, jnp.concatenate(halves(vortex_ref[...].reshape(rows, N)), 0))
    modal = modal[:rows] + modal[rows:]
    mirror = mirrored(modal[:, HALF:])
    folded = [halves(modal[:, :HALF] + mirror), halves(modal[:, :HALF] - mirror)]
    for n in range(PIECES):
        cols = slice(n * STEP, (n + 1) * STEP)
        odd, start = divmod(n * STEP, HALF)
        if start == 0:
            wait(waves[4 * odd : 4 * odd + 4])
            if odd:
                written += fetch([(vortex_ref, carry_hbm.at[pl.ds(2 * TALL, NL)])], sems, 16 + PIECES)
        some = slice(start, start + STEP)
        spectrum = split_dot(folded[odd], (table_ref[odd, 0, :, some], table_ref[odd, 1, :, some]))
        right = jnp.zeros((NL, STEP), jnp.float32)
        left = jnp.zeros((NL, STEP), jnp.float32)
        force = []
        for y in range(ROWS):
            force.append(-weight[:, cols] * spectrum[y * NL : (y + 1) * NL])
            force_ref[2 * y : 2 * y + 2, :, cols] = force[y].reshape(2, ROWS, STEP)
            right = rho[:, cols] * right + force[y]
        for y in reversed(range(ROWS)):
            left = rho[:, cols] * left + force[y]
        for c in range(STEP // LANES):
            dest = n * (STEP // LANES) + c
            part = slice(c * LANES, (c + 1) * LANES)
            send_ref[dest * NL : (dest + 1) * NL, 0, :LANES] = right[:, part]
            send_ref[dest * NL : (dest + 1) * NL, 0, LANES : 2 * LANES] = left[:, part]
            part = slice(dest * LANES, (dest + 1) * LANES)
            send_ref[dest * NL : (dest + 1) * NL, 0, 2 * LANES : 3 * LANES] = vortex_ref[:, ROWS - 1, part]
            send_ref[dest * NL : (dest + 1) * NL, 0, 3 * LANES :] = vortex_ref[:, 0, part]
        dests = pl.ds(n * (STEP // LANES) * NL, STEP // LANES * NL)
        written += fetch([(send_ref.at[dests], send_hbm.at[dests])], sems, 15 + n)
    wait(copies[2:])
    force_ref[2 * ROWS + 2 :, :, :NL] = back_ref[...].reshape(2, ROWS, NL)
    written += fetch([(force_ref, carry_hbm.at[pl.ds(0, 2 * TALL)])], sems, 15 + PIECES)
    wait(written)


def shift_rows(value, step):
    blank = jnp.zeros((abs(step), value.shape[1]), value.dtype)
    if step > 0:
        return jnp.concatenate([blank, value[:-step]], 0)
    return jnp.concatenate([value[-step:], blank], 0)


def scan_kernel(take_ref, ends_ref, give_hbm, give_ref, sems):
    rates = [ends_ref[2 * BLOCKS + bit : 2 * BLOCKS + bit + 1] for bit in range(8)]
    rho = ends_ref[2 * BLOCKS + 8 : 2 * BLOCKS + 9]
    right = take_ref[:, 0, :LANES]
    left = take_ref[:, 0, LANES : 2 * LANES]
    for bit, rate in enumerate(rates[:-1]):
        right = right + rate * shift_rows(right, 1 << bit)
        left = left + rate * shift_rows(left, -1 << bit)
    below = rho * left[:1]
    above = rho * right[BLOCKS - 1 :]
    far = rates[-1] * rho
    scale = 1.0 / (1.0 - far * far)
    alpha = -(below - far * above) * scale
    beta = -(above - far * below) * scale
    give_ref[:, 0, :LANES] = shift_rows(right, 1) + alpha * ends_ref[:BLOCKS]
    give_ref[:, 0, LANES : 2 * LANES] = shift_rows(left, -1) + beta * ends_ref[BLOCKS : 2 * BLOCKS]
    give_ref[:, 0, 2 * LANES : 3 * LANES] = shift_rows(take_ref[:, 0, 2 * LANES : 3 * LANES], 1)
    give_ref[:, 0, 3 * LANES :] = shift_rows(take_ref[:, 0, 3 * LANES :], -1)
    wait(fetch([(give_ref, give_hbm)], sems))


def part_kernel(
    index_ref, carry_hbm, part_ref, mixed_ref, ends_ref, force_ref, sems
):
    wait(fetch([(carry_hbm.at[pl.ds(0, 2 * TALL)], force_ref)], sems))
    me = index_ref[0]
    here = pl.ds(pl.multiple_of(me // NL * LANES, LANES), LANES)
    every = force_ref[2 * ROWS : 2 * ROWS + 2, :, here].reshape(NL, LANES)
    rho = jnp.sum(jnp.where(iota((NL, LANES), 0) == me % NL, every, 0.0), 0, keepdims=True)
    rate = rho
    for _ in range(3):
        rate = rate * rate
    place = iota((BLOCKS, LANES), 0)
    power = jnp.ones((BLOCKS, LANES), jnp.float32)
    reverse = power
    for bit in range(8):
        ends_ref[2 * BLOCKS + bit : 2 * BLOCKS + bit + 1] = rate
        if bit < 7:
            odd = (place >> bit) % 2 == 1
            power = power * jnp.where(odd, rate, 1.0)
            reverse = reverse * jnp.where(odd, 1.0, rate)
        rate = rate * rate
    ends_ref[2 * BLOCKS + 8 : 2 * BLOCKS + 9] = rho
    ends_ref[:BLOCKS] = power
    ends_ref[BLOCKS : 2 * BLOCKS] = reverse
    tall = NL * TALL
    row = iota((tall, NL), 0)
    layer = jnp.where(row < NL * ROWS, row // ROWS, row % NL)
    pick = (layer == iota((tall, NL), 1)).astype(jnp.float32)
    wide = (iota((NL, tall), 1) % NL == iota((NL, tall), 0)).astype(jnp.float32)
    mixed = dot(dot(pick, force_ref[2 * ROWS + 2 :, :, :NL].reshape(NL, NL), HIGHEST), wide, HIGHEST)
    row = iota((tall, tall), 0)
    place = jnp.where(row < NL * ROWS, row % ROWS + 1, jnp.where(row < NL * (ROWS + 1), 0, ROWS + 1))
    mixed_ref[...] = jnp.where(iota((tall, tall), 1) // NL == place, mixed, 0.0)
    force = [force_ref[2 * y : 2 * y + 2].reshape(NL, N) for y in range(ROWS + 1)]
    rho = force[ROWS]
    part_ref[TALL] = rho
    right = jnp.zeros((NL, N), jnp.float32)
    for y in range(ROWS):
        right = rho * right + force[y]
        part_ref[y + 1] = right
    part_ref[ROWS + 1] = rho * right
    left = jnp.zeros((NL, N), jnp.float32)
    for y in reversed(range(ROWS)):
        part_ref[y + 1] += left
        left = rho * (left + force[y])
    part_ref[0] = left


def roll_lanes(value, step):
    width = value.shape[1]
    lane = iota(value.shape, 1)
    rolled = pltpu.roll(value, step % width, 1)
    return jnp.where(lane == (0 if step > 0 else width - 1), 0.0, rolled)


def roll_sub(value, edge, step):
    height = value.shape[0]
    sub = iota(value.shape, 0)
    rolled = pltpu.roll(value, step % height, 0)
    return jnp.where(sub == (0 if step > 0 else height - 1), edge, rolled)


def difference(value):
    return roll_lanes(value, -1) - roll_lanes(value, 1)


def backward_kernel(
    index_ref, take_ref, part_ref, mixed_ref, table_ref, wet_ref, wind_ref, carry_hbm, vortex_hbm, stream_hbm, given_ref, psi_ref,
    south_ref, north_ref, edge_ref, wave_ref, vortex_ref, stream_ref, sems,
):
    loads = fetch(
        [(carry_hbm.at[pl.ds(2 * TALL + i, 4)], given_ref.at[pl.ds(i, 4)]) for i in range(0, NL, 4)], sems
    )
    out = len(loads)
    for c in range(N // LANES):
        cols = slice(c * LANES, (c + 1) * LANES)
        up = take_ref[c * NL : (c + 1) * NL, 0, :LANES]
        down = take_ref[c * NL : (c + 1) * NL, 0, LANES : 2 * LANES]
        south_ref[:, cols] = take_ref[c * NL : (c + 1) * NL, 0, 2 * LANES : 3 * LANES]
        north_ref[:, cols] = take_ref[c * NL : (c + 1) * NL, 0, 3 * LANES :]
        near = part_ref[TALL, :, cols]
        ups, downs = [up], [down]
        for _ in range(ROWS + 1):
            ups.append(ups[-1] * near)
            downs.append(downs[-1] * near)
        for i in range(TALL):
            psi_ref[i * NL : (i + 1) * NL, cols] = part_ref[i, :, cols] + ups[i] + downs[ROWS + 1 - i]
    split = halves(split_dot(halves(mixed_ref[...]), halves(psi_ref[...])))
    sums = []
    for odd in range(2):
        some = tuple(part[:, odd * HALF : (odd + 1) * HALF] for part in split)
        sums.append(split_dot(some, (table_ref[odd, 0], table_ref[odd, 1]), 1))
    wave_ref[:, :HALF] = sums[0] + sums[1]
    wave_ref[:, HALF:] = mirrored(sums[0] - sums[1])
    inside_low = jnp.where(index_ref[0] > 0, 1.0, 0.0)
    inside_high = jnp.where(index_ref[0] < BLOCKS - 1, 1.0, 0.0)
    body = NL * ROWS
    for layer in range(NL):
        stream_ref[layer] = wave_ref[layer * ROWS : (layer + 1) * ROWS]
    written = fetch([(stream_ref, stream_hbm)], sems, out)
    wait(loads)
    keep = time_step * wet_ref[...].astype(jnp.float32)
    twelfth = keep * (1.0 / 12.0)
    edges = [inside_low * wave_ref[body : body + NL], inside_high * wave_ref[body + NL :], south_ref[...], north_ref[...]]
    for i, edge in enumerate(edges):
        edge_ref[2 * i] = edge
        edge_ref[2 * i + 1] = difference(edge)
    for layer in range(NL):
        below, across_below, above, across_above, old_below, old_across_below, old_above, old_across_above = (
            edge_ref[i, layer : layer + 1] for i in range(8)
        )
        old = given_ref[layer]
        old_across = difference(old)
        old_north = roll_sub(old, old_above, -1)
        old_south = roll_sub(old, old_below, 1)
        mid = stream_ref[layer]
        east, west = roll_lanes(mid, -1), roll_lanes(mid, 1)
        across = east - west
        north = roll_sub(mid, above, -1)
        south = roll_sub(mid, below, 1)
        along = north - south
        mixture = (old_north - old_south + 12.0 * 0.5 * beta_plane) * mid - old * along
        total = old_south * (across + roll_sub(across, across_below, 1))
        total -= old_north * (across + roll_sub(across, across_above, -1))
        total += old_across * along - difference(mixture)
        total += roll_sub(old_across, old_across_above, -1) * north - roll_sub(old_across, old_across_below, 1) * south
        total = old + twelfth * total
        if layer == 0:
            total += keep * wind_ref[...]
        if layer == NL - 1:
            total -= (bottom_drag * keep) * (north + south + east + west - 4.0 * mid)
        vortex_ref[layer] = total
        if layer % 4 == 3:
            some = slice(layer - 3, layer + 1)
            written += fetch([(vortex_ref.at[some], vortex_hbm.at[some])], sems, out + 1 + layer // 4)
    wait(written)


def call(kernel, outs, args, scratch, flops, nbytes, scalars=(), near=(), limit=60 * 1024 * 1024, kept=0):
    def room(kind):
        return pltpu.VMEM(*kind) if isinstance(kind, tuple) else kind

    return pl.pallas_call(
        kernel,
        out_shape=[jax.ShapeDtypeStruct(s, d) for s, d in outs],
        in_specs=[SMEM] * len(scalars) + [VMEM] * len(near) + [ANY] * len(args),
        out_specs=[ANY] * (len(outs) - kept) + [VMEM] * kept,
        scratch_shapes=[room(kind) for kind in scratch],
        compiler_params=pltpu.CompilerParams(vmem_limit_bytes=limit),
        cost_estimate=pl.CostEstimate(flops=flops, bytes_accessed=nbytes, transcendentals=0),
    )(*scalars, *near, *args)


def body(vorticity, layer_to_mode, mode_to_layer, inverse_radii, wind_curl, wet_mask):
    field = ((NL, ROWS, N), f32)
    plane = ((ROWS, N), f32)
    edge = ((NL, N), f32)
    mixing = ((NL, NL), f32)
    sines = ((2, 2, HALF, HALF), bf16)
    packet = ((BLOCKS, 1, 4 * LANES), f32)
    rows = ((2 * TALL, ROWS, N), f32)
    carry = ((112, ROWS, N), f32)
    rates = pltpu.SMEM((NL,), f32)
    parts = [((TALL + 1, NL, N), f32), ((NL * TALL, NL * TALL), f32)]
    ends = ((2 * BLOCKS + 16, LANES), f32)
    wave = ((NL * TALL, N), f32)

    index = (lax.axis_index("group") * lax.axis_size("tile") + lax.axis_index("tile")).astype(i32).reshape(1)
    outs = [packet, carry]
    table = jnp.asarray(host_table())
    send, kept = call(
        forward_kernel, outs, (vorticity, layer_to_mode, mode_to_layer, inverse_radii, table),
        [field, mixing, mixing, rates, sines, packet, rows, DMA((17 + PIECES,))],
        6 * 128 * N * N, 6 << 20, limit=64000 << 10,
    )
    take = lax.all_to_all(send, AXES, split_axis=0, concat_axis=0, tiled=True)
    part, mixed, ends = call(
        part_kernel, [*parts, ends], (kept,), [rows, DMA((1,))], 1 << 24, 1 << 20, [index], limit=50000 << 10, kept=3
    )
    (give,) = call(
        scan_kernel, [packet], (), [packet, DMA((1,))], 1 << 22, 1 << 18, (), [take, ends], limit=54500 << 10,
    )
    amplitude = lax.all_to_all(give, AXES, split_axis=0, concat_axis=0, tiled=True)
    return tuple(
        call(
            backward_kernel, [field, field],
            (kept,), [field, wave, edge, edge, ((8, NL, N), f32), wave, field, field, DMA((9,))],
            6 * 160 * N * N, 6 << 20, [index], [amplitude, part, mixed, table, wet_mask, wind_curl], limit=51500 << 10,
        )
    )


def solution(mesh):
    rows = P(None, AXES, None)
    return jax.shard_map(
        body,
        mesh=mesh,
        in_specs=(rows, P(), P(), P(), P(AXES, None), P(AXES, None)),
        out_specs=(rows, rows),
        check_vma=False,
    )
```

```python
import math

import jax
import jax.numpy as jnp
import numpy as np
from jax import lax
from jax.experimental import pallas as pl
from jax.experimental.pallas import tpu as pltpu
from jax.sharding import PartitionSpec as P

time_step = 0.5
beta_plane = 1.0
bottom_drag = 0.2

N = 1024
NL = 16
ROWS = 8
TALL = ROWS + 2
BLOCKS = 128
LANES = 128
HALF = N // 2
STEP = 256
PIECES = N // STEP
AXES = ("group", "tile")
HIGHEST = lax.Precision.HIGHEST
SMEM = pl.BlockSpec(memory_space=pltpu.SMEM)
VMEM = pl.BlockSpec(memory_space=pltpu.VMEM)
ANY = pl.BlockSpec(memory_space=pl.ANY)
DMA = pltpu.SemaphoreType.DMA
f32, bf16, i32 = jnp.float32, jnp.bfloat16, jnp.int32


def host_table():
    k = np.arange(1, N + 1)
    sine = math.sqrt(2.0 / (N + 1)) * np.sin(np.pi * ((k[:, None] * k[None, :]) % (2 * (N + 1))) / (N + 1))
    table = np.stack([sine[:HALF, 0::2], sine[:HALF, 1::2]])
    high = table.astype(jnp.bfloat16)
    low = (table - high.astype(np.float64)).astype(jnp.bfloat16)
    return np.stack([high, low], 1)


def host_waves():
    found = []
    for odd in range(2):
        wave = np.arange(1 + odd, N + 1, 2)
        angle_a, angle_b = (
            np.pi * ((place[:, None] * wave[None, :]) % (2 * (N + 1))) / (N + 1)
            for place in (32 * np.arange(16), np.arange(1, 33))
        )
        scale = math.sqrt(2.0 / (N + 1))
        rows = [np.sin(angle_a), np.cos(angle_a), scale * np.sin(angle_b), scale * np.cos(angle_b)]
        found.append(np.concatenate(rows, 0).reshape(3, 32, HALF))
    return np.stack(found).astype(np.float32)


def iota(shape, dim):
    return lax.broadcasted_iota(jnp.int32, shape, dim)


def dot(left, right, precision=None, across=0):
    return lax.dot_general(
        left, right, (((1,), (across,)), ((), ())), precision=precision, preferred_element_type=jnp.float32
    )


def halves(value):
    high = value.astype(jnp.bfloat16)
    low = (value - high.astype(jnp.float32)).astype(jnp.bfloat16)
    return high, low


def split_dot(left, right, across=0):
    count = left[0].shape[0]
    both = dot(jnp.concatenate(left, 0), right[0], None, across)
    return both[:count] + both[count:] + dot(left[0], right[1], None, across)


def mirrored(value):
    flip = (iota((STEP, STEP), 0) + iota((STEP, STEP), 1) == STEP - 1).astype(jnp.bfloat16)
    count, width = value.shape
    parts = jnp.concatenate(halves(value), 0)
    blocks = [dot(parts[:, i : i + STEP], flip) for i in range(0, width, STEP)]
    return jnp.concatenate([block[:count] + block[count:] for block in reversed(blocks)], 1)


def fetch(pairs, sems, first=0):
    copies = [pltpu.make_async_copy(src, dst, sems.at[first + i]) for i, (src, dst) in enumerate(pairs)]
    for copy in copies:
        copy.start()
    return copies


def wait(copies):
    for copy in copies:
        copy.wait()


def eigen_values(first, width):
    column = iota((1, width), 1) + first
    wave = jnp.where(column < HALF, 2 * column + 1, 2 * column + 2 - N).astype(jnp.float32)
    angle = wave * (math.pi / (2 * (N + 1)))
    square = angle * angle
    series = jnp.full_like(square, 1.0 / math.factorial(15))
    for order in (13, 11, 9, 7, 5, 3, 1):
        series = 1.0 / math.factorial(order) - square * series
    sine = angle * series
    return 4.0 * sine * sine


def radii_column(radii_ref, shape):
    sub = iota(shape, 0)
    column = jnp.zeros(shape, jnp.float32)
    for m in range(NL):
        column = jnp.where(sub == m, radii_ref[m], column)
    return column


def decay_of(shift):
    half = 0.5 * jnp.sqrt(shift)
    root = jnp.sqrt(1.0 + 0.25 * shift)
    grow = half + root
    return 1.0 / (grow * grow), 1.0 / (4.0 * half * root)


def mode_decay(radii_ref):
    return decay_of(eigen_values(0, N) + radii_column(radii_ref, (NL, N)))


def forward_kernel(
    vortex_hbm, mix_hbm, back_hbm, radii_hbm, wave_hbm,
    send_hbm, carry_hbm,
    vortex_ref, mix_ref, back_ref, radii_ref, wave_ref, table_ref, send_ref, force_ref, sems,
):
    copies = fetch([(mix_hbm, mix_ref), (radii_hbm, radii_ref)], sems)
    layers = [pl.ds(i, 4) for i in range(0, NL, 4)]
    loads = fetch([(vortex_hbm.at[some], vortex_ref.at[some]) for some in layers], sems, 2)
    copies += fetch([(back_hbm, back_ref)], sems, 6)
    waves = fetch([(wave_hbm.at[i], wave_ref.at[i]) for i in range(2)], sems, 7)
    rows = NL * ROWS
    spread = (iota((NL, rows), 1) // ROWS == iota((NL, rows), 0)).astype(jnp.float32)
    wait(copies[:2])
    rho, weight = mode_decay(radii_ref)
    force_ref[2 * ROWS : 2 * ROWS + 2] = rho.reshape(2, ROWS, N)
    wide = dot(mix_ref[...], spread, HIGHEST)
    mix = jnp.concatenate([wide] * ROWS, 0)
    mix = jnp.where(iota((rows, rows), 0) // NL == iota((rows, rows), 1) % ROWS, mix, 0.0)
    wait(loads + waves)
    written = fetch([(vortex_ref, carry_hbm.at[pl.ds(2 * TALL, NL)])], sems, 16 + PIECES)
    high, low = halves(mix)
    mix = jnp.concatenate([jnp.concatenate([high, high], 1), jnp.concatenate([low, jnp.zeros_like(low)], 1)], 0)
    modal = dot(mix, jnp.concatenate(halves(vortex_ref[...].reshape(rows, N)), 0))
    modal = modal[:rows] + modal[rows:]
    wait(copies[2:])
    force_ref[2 * ROWS + 2 :, :, :NL] = back_ref[...].reshape(2, ROWS, NL)
    rest = pl.ds(2 * ROWS, 4)
    written += fetch([(force_ref.at[rest], carry_hbm.at[rest])], sems, 15 + PIECES)
    mirror = mirrored(modal[:, HALF:])
    folded = [halves(modal[:, :HALF] + mirror), halves(modal[:, :HALF] - mirror)]
    for n in range(PIECES):
        cols = slice(n * STEP, (n + 1) * STEP)
        odd, start = divmod(n * STEP, HALF)
        if start == 0:
            for a in range(16):
                block = wave_ref[odd, 0, a : a + 1] * wave_ref[odd, 2]
                block += wave_ref[odd, 0, 16 + a : 17 + a] * wave_ref[odd, 1]
                high, low = halves(block)
                table_ref[odd, 0, 32 * a : 32 * a + 32] = high
                table_ref[odd, 1, 32 * a : 32 * a + 32] = low
        some = slice(start, start + STEP)
        spectrum = split_dot(folded[odd], (table_ref[odd, 0, :, some], table_ref[odd, 1, :, some]))
        right = jnp.zeros((NL, STEP), jnp.float32)
        left = jnp.zeros((NL, STEP), jnp.float32)
        force = []
        for y in range(ROWS):
            force.append(-weight[:, cols] * spectrum[y * NL : (y + 1) * NL])
            force_ref[2 * y : 2 * y + 2, :, cols] = force[y].reshape(2, ROWS, STEP)
            right = rho[:, cols] * right + force[y]
        for y in reversed(range(ROWS)):
            left = rho[:, cols] * left + force[y]
        for c in range(STEP // LANES):
            dest = n * (STEP // LANES) + c
            part = slice(c * LANES, (c + 1) * LANES)
            send_ref[dest * NL : (dest + 1) * NL, 0, :LANES] = right[:, part]
            send_ref[dest * NL : (dest + 1) * NL, 0, LANES : 2 * LANES] = left[:, part]
            part = slice(dest * LANES, (dest + 1) * LANES)
            send_ref[dest * NL : (dest + 1) * NL, 0, 2 * LANES : 3 * LANES] = vortex_ref[:, ROWS - 1, part]
            send_ref[dest * NL : (dest + 1) * NL, 0, 3 * LANES :] = vortex_ref[:, 0, part]
        dests = pl.ds(n * (STEP // LANES) * NL, STEP // LANES * NL)
        written += fetch([(send_ref.at[dests], send_hbm.at[dests])], sems, 15 + n)
        some = pl.ds(0, 2 * ROWS), slice(None), pl.ds(n * STEP, STEP)
        written += fetch([(force_ref.at[some], carry_hbm.at[some])], sems, 17 + PIECES + n)
    wait(written)


def shift_rows(value, step):
    blank = jnp.zeros((abs(step), value.shape[1]), value.dtype)
    if step > 0:
        return jnp.concatenate([blank, value[:-step]], 0)
    return jnp.concatenate([value[-step:], blank], 0)


def scan_kernel(take_ref, ends_ref, give_hbm, give_ref, sems):
    rates = [ends_ref[2 * BLOCKS + bit : 2 * BLOCKS + bit + 1] for bit in range(8)]
    rho = ends_ref[2 * BLOCKS + 8 : 2 * BLOCKS + 9]
    right = take_ref[:, 0, :LANES]
    left = take_ref[:, 0, LANES : 2 * LANES]
    for bit, rate in enumerate(rates[:-1]):
        right = right + rate * shift_rows(right, 1 << bit)
        left = left + rate * shift_rows(left, -1 << bit)
    below = rho * left[:1]
    above = rho * right[BLOCKS - 1 :]
    far = rates[-1] * rho
    scale = 1.0 / (1.0 - far * far)
    alpha = -(below - far * above) * scale
    beta = -(above - far * below) * scale
    give_ref[:, 0, :LANES] = shift_rows(right, 1) + alpha * ends_ref[:BLOCKS]
    give_ref[:, 0, LANES : 2 * LANES] = shift_rows(left, -1) + beta * ends_ref[BLOCKS : 2 * BLOCKS]
    give_ref[:, 0, 2 * LANES : 3 * LANES] = shift_rows(take_ref[:, 0, 2 * LANES : 3 * LANES], 1)
    give_ref[:, 0, 3 * LANES :] = shift_rows(take_ref[:, 0, 3 * LANES :], -1)
    wait(fetch([(give_ref, give_hbm)], sems))


def part_kernel(
    index_ref, carry_hbm, part_ref, mixed_ref, ends_ref, force_ref, sems
):
    wait(fetch([(carry_hbm.at[pl.ds(0, 2 * TALL)], force_ref)], sems))
    me = index_ref[0]
    here = pl.ds(pl.multiple_of(me // NL * LANES, LANES), LANES)
    every = force_ref[2 * ROWS : 2 * ROWS + 2, :, here].reshape(NL, LANES)
    rho = jnp.sum(jnp.where(iota((NL, LANES), 0) == me % NL, every, 0.0), 0, keepdims=True)
    rate = rho
    for _ in range(3):
        rate = rate * rate
    place = iota((BLOCKS, LANES), 0)
    power = jnp.ones((BLOCKS, LANES), jnp.float32)
    reverse = power
    for bit in range(8):
        ends_ref[2 * BLOCKS + bit : 2 * BLOCKS + bit + 1] = rate
        if bit < 7:
            odd = (place >> bit) % 2 == 1
            power = power * jnp.where(odd, rate, 1.0)
            reverse = reverse * jnp.where(odd, 1.0, rate)
        rate = rate * rate
    ends_ref[2 * BLOCKS + 8 : 2 * BLOCKS + 9] = rho
    ends_ref[:BLOCKS] = power
    ends_ref[BLOCKS : 2 * BLOCKS] = reverse
    tall = NL * TALL
    row = iota((tall, NL), 0)
    layer = jnp.where(row < NL * ROWS, row // ROWS, row % NL)
    pick = (layer == iota((tall, NL), 1)).astype(jnp.float32)
    wide = (iota((NL, tall), 1) % NL == iota((NL, tall), 0)).astype(jnp.float32)
    mixed = dot(dot(pick, force_ref[2 * ROWS + 2 :, :, :NL].reshape(NL, NL), HIGHEST), wide, HIGHEST)
    row = iota((tall, tall), 0)
    place = jnp.where(row < NL * ROWS, row % ROWS + 1, jnp.where(row < NL * (ROWS + 1), 0, ROWS + 1))
    mixed_ref[...] = jnp.where(iota((tall, tall), 1) // NL == place, mixed, 0.0)
    force = [force_ref[2 * y : 2 * y + 2].reshape(NL, N) for y in range(ROWS + 1)]
    rho = force[ROWS]
    part_ref[TALL] = rho
    right = jnp.zeros((NL, N), jnp.float32)
    for y in range(ROWS):
        right = rho * right + force[y]
        part_ref[y + 1] = right
    part_ref[ROWS + 1] = rho * right
    left = jnp.zeros((NL, N), jnp.float32)
    for y in reversed(range(ROWS)):
        part_ref[y + 1] += left
        left = rho * (left + force[y])
    part_ref[0] = left


def roll_lanes(value, step):
    width = value.shape[1]
    rolled = pltpu.roll(value, step % width, 1)
    lane = iota((value.shape[0], LANES), 1)
    if step > 0:
        edge = jnp.where(lane == 0, 0.0, rolled[:, :LANES])
        return jnp.concatenate([edge, rolled[:, LANES:]], 1)
    edge = jnp.where(lane == LANES - 1, 0.0, rolled[:, -LANES:])
    return jnp.concatenate([rolled[:, :-LANES], edge], 1)


def roll_sub(value, edge, step):
    height = value.shape[0]
    sub = iota(value.shape, 0)
    rolled = pltpu.roll(value, step % height, 0)
    return jnp.where(sub == (0 if step > 0 else height - 1), edge, rolled)


def difference(value):
    return roll_lanes(value, -1) - roll_lanes(value, 1)


def backward_kernel(
    index_ref, take_ref, part_ref, mixed_ref, table_ref, wet_ref, wind_ref, carry_hbm, vortex_hbm, stream_hbm, given_ref, psi_ref,
    south_ref, north_ref, edge_ref, wave_ref, vortex_ref, stream_ref, sems,
):
    loads = fetch(
        [(carry_hbm.at[pl.ds(2 * TALL + i, 4)], given_ref.at[pl.ds(i, 4)]) for i in range(0, NL, 4)], sems
    )
    out = len(loads)
    for c in range(N // LANES):
        cols = slice(c * LANES, (c + 1) * LANES)
        up = take_ref[c * NL : (c + 1) * NL, 0, :LANES]
        down = take_ref[c * NL : (c + 1) * NL, 0, LANES : 2 * LANES]
        south_ref[:, cols] = take_ref[c * NL : (c + 1) * NL, 0, 2 * LANES : 3 * LANES]
        north_ref[:, cols] = take_ref[c * NL : (c + 1) * NL, 0, 3 * LANES :]
        near = part_ref[TALL, :, cols]
        ups, downs = [up], [down]
        for _ in range(ROWS + 1):
            ups.append(ups[-1] * near)
            downs.append(downs[-1] * near)
        for i in range(TALL):
            psi_ref[i * NL : (i + 1) * NL, cols] = part_ref[i, :, cols] + ups[i] + downs[ROWS + 1 - i]
    split = halves(split_dot(halves(mixed_ref[...]), halves(psi_ref[...])))
    sums = []
    for odd in range(2):
        some = tuple(part[:, odd * HALF : (odd + 1) * HALF] for part in split)
        sums.append(split_dot(some, (table_ref[odd, 0], table_ref[odd, 1]), 1))
    wave_ref[:, :HALF] = sums[0] + sums[1]
    wave_ref[:, HALF:] = mirrored(sums[0] - sums[1])
    inside_low = jnp.where(index_ref[0] > 0, 1.0, 0.0)
    inside_high = jnp.where(index_ref[0] < BLOCKS - 1, 1.0, 0.0)
    body = NL * ROWS
    for layer in range(NL):
        stream_ref[layer] = wave_ref[layer * ROWS : (layer + 1) * ROWS]
    written = fetch([(stream_ref, stream_hbm)], sems, out)
    wait(loads)
    keep = time_step * wet_ref[...].astype(jnp.float32)
    twelfth = keep * (1.0 / 12.0)
    streams = inside_low * wave_ref[body : body + NL], inside_high * wave_ref[body + NL :]
    for side, (stream, old) in enumerate(zip(streams, (south_ref[...], north_ref[...]))):
        edge_ref[3 * side] = stream
        edge_ref[3 * side + 1] = old
        edge_ref[3 * side + 2] = difference(old) * stream - old * difference(stream)
    for layer in range(NL):
        rows = [edge_ref[i, layer : layer + 1] for i in range(6)]

        def rise(value, i):
            return roll_sub(value, rows[3 + i], -1) - roll_sub(value, rows[i], 1)

        mid = stream_ref[layer]
        old = given_ref[layer]
        east, west = roll_lanes(mid, -1), roll_lanes(mid, 1)
        across, along = east - west, rise(mid, 0)
        old_across, old_along = difference(old), rise(old, 1)
        total = old_across * along - old_along * across
        total += rise(old_across * mid - old * across, 2)
        total -= difference((old_along + 12.0 * 0.5 * beta_plane) * mid - old * along)
        total = old + twelfth * total
        if layer == 0:
            total += keep * wind_ref[...]
        if layer == NL - 1:
            both = roll_sub(mid, rows[3], -1) + roll_sub(mid, rows[0], 1)
            total -= (bottom_drag * keep) * (both + east + west - 4.0 * mid)
        vortex_ref[layer] = total
        if layer % 4 == 3:
            some = slice(layer - 3, layer + 1)
            written += fetch([(vortex_ref.at[some], vortex_hbm.at[some])], sems, out + 1 + layer // 4)
    wait(written)


def call(kernel, outs, args, scratch, flops, nbytes, scalars=(), near=(), limit=60 * 1024 * 1024, kept=0):
    def room(kind):
        return pltpu.VMEM(*kind) if isinstance(kind, tuple) else kind

    return pl.pallas_call(
        kernel,
        out_shape=[jax.ShapeDtypeStruct(s, d) for s, d in outs],
        in_specs=[SMEM] * len(scalars) + [VMEM] * len(near) + [ANY] * len(args),
        out_specs=[ANY] * (len(outs) - kept) + [VMEM] * kept,
        scratch_shapes=[room(kind) for kind in scratch],
        compiler_params=pltpu.CompilerParams(vmem_limit_bytes=limit),
        cost_estimate=pl.CostEstimate(flops=flops, bytes_accessed=nbytes, transcendentals=0),
    )(*scalars, *near, *args)


def body(vorticity, layer_to_mode, mode_to_layer, inverse_radii, wind_curl, wet_mask):
    field = ((NL, ROWS, N), f32)
    plane = ((ROWS, N), f32)
    edge = ((NL, N), f32)
    mixing = ((NL, NL), f32)
    sines = ((2, 2, HALF, HALF), bf16)
    packet = ((BLOCKS, 1, 4 * LANES), f32)
    rows = ((2 * TALL, ROWS, N), f32)
    carry = ((112, ROWS, N), f32)
    rates = pltpu.SMEM((NL,), f32)
    parts = [((TALL + 1, NL, N), f32), ((NL * TALL, NL * TALL), f32)]
    ends = ((2 * BLOCKS + 16, LANES), f32)
    wave = ((NL * TALL, N), f32)

    index = (lax.axis_index("group") * lax.axis_size("tile") + lax.axis_index("tile")).astype(i32).reshape(1)
    outs = [packet, carry]
    table = jnp.asarray(host_table())
    send, kept = call(
        forward_kernel, outs, (vorticity, layer_to_mode, mode_to_layer, inverse_radii, jnp.asarray(host_waves())),
        [field, mixing, mixing, rates, ((2, 3, 32, HALF), f32), sines, packet, rows, DMA((17 + 2 * PIECES,))],
        6 * 128 * N * N, 6 << 20, limit=64000 << 10,
    )
    take = lax.all_to_all(send, AXES, split_axis=0, concat_axis=0, tiled=True)
    part, mixed, ends = call(
        part_kernel, [*parts, ends], (kept,), [rows, DMA((1,))], 1 << 24, 1 << 20, [index], limit=50000 << 10, kept=3
    )
    (give,) = call(
        scan_kernel, [packet], (), [packet, DMA((1,))], 1 << 22, 1 << 18, (), [take, ends], limit=54500 << 10,
    )
    amplitude = lax.all_to_all(give, AXES, split_axis=0, concat_axis=0, tiled=True)
    return tuple(
        call(
            backward_kernel, [field, field],
            (kept,), [field, wave, edge, edge, ((6, NL, N), f32), wave, field, field, DMA((9,))],
            6 * 160 * N * N, 6 << 20, [index], [amplitude, part, mixed, table, wet_mask, wind_curl], limit=51500 << 10,
        )
    )


def solution(mesh):
    rows = P(None, AXES, None)
    return jax.shard_map(
        body,
        mesh=mesh,
        in_specs=(rows, P(), P(), P(), P(AXES, None), P(AXES, None)),
        out_specs=(rows, rows),
        check_vma=False,
    )
```

```python
import math

import jax
import jax.numpy as jnp
import numpy as np
from jax import lax
from jax.experimental import pallas as pl
from jax.experimental.pallas import tpu as pltpu
from jax.sharding import PartitionSpec as P

time_step = 0.5
beta_plane = 1.0
bottom_drag = 0.2

N = 1024
NL = 16
ROWS = 8
TALL = ROWS + 2
BLOCKS = 128
LANES = 128
HALF = N // 2
STEP = 256
PIECES = N // STEP
AXES = ("group", "tile")
HIGHEST = lax.Precision.HIGHEST
SMEM = pl.BlockSpec(memory_space=pltpu.SMEM)
VMEM = pl.BlockSpec(memory_space=pltpu.VMEM)
ANY = pl.BlockSpec(memory_space=pl.ANY)
DMA = pltpu.SemaphoreType.DMA
f32, bf16, i32 = jnp.float32, jnp.bfloat16, jnp.int32


def host_table():
    k = np.arange(1, N + 1)
    sine = math.sqrt(2.0 / (N + 1)) * np.sin(np.pi * ((k[:, None] * k[None, :]) % (2 * (N + 1))) / (N + 1))
    table = np.stack([sine[:HALF, 0::2], sine[:HALF, 1::2]])
    high = table.astype(jnp.bfloat16)
    low = (table - high.astype(np.float64)).astype(jnp.bfloat16)
    return np.stack([high, low], 1)


def host_waves():
    found = []
    for odd in range(2):
        wave = np.arange(1 + odd, N + 1, 2)
        angle_a, angle_b = (
            np.pi * ((place[:, None] * wave[None, :]) % (2 * (N + 1))) / (N + 1)
            for place in (32 * np.arange(16), np.arange(1, 33))
        )
        scale = math.sqrt(2.0 / (N + 1))
        rows = [np.sin(angle_a), np.cos(angle_a), scale * np.sin(angle_b), scale * np.cos(angle_b)]
        found.append(np.concatenate(rows, 0).reshape(3, 32, HALF))
    return np.stack(found).astype(np.float32)


def iota(shape, dim):
    return lax.broadcasted_iota(jnp.int32, shape, dim)


def dot(left, right, precision=None, across=0):
    return lax.dot_general(
        left, right, (((1,), (across,)), ((), ())), precision=precision, preferred_element_type=jnp.float32
    )


def halves(value):
    high = value.astype(jnp.bfloat16)
    low = (value - high.astype(jnp.float32)).astype(jnp.bfloat16)
    return high, low


def split_dot(left, right, across=0):
    count = left[0].shape[0]
    both = dot(jnp.concatenate(left, 0), right[0], None, across)
    return both[:count] + both[count:] + dot(left[0], right[1], None, across)


def mirrored(value, third=False):
    flip = (iota((STEP, STEP), 0) + iota((STEP, STEP), 1) == STEP - 1).astype(jnp.bfloat16)
    count, width = value.shape
    parts = list(halves(value))
    if third:
        rest = value - parts[0].astype(jnp.float32) - parts[1].astype(jnp.float32)
        parts.append(rest.astype(jnp.bfloat16))
    stack = jnp.concatenate(parts, 0)
    blocks = []
    for i in reversed(range(0, width, STEP)):
        block = dot(stack[:, i : i + STEP], flip)
        blocks.append(sum(block[j * count : (j + 1) * count] for j in reversed(range(len(parts)))))
    return jnp.concatenate(blocks, 1)


def fetch(pairs, sems, first=0):
    copies = [pltpu.make_async_copy(src, dst, sems.at[first + i]) for i, (src, dst) in enumerate(pairs)]
    for copy in copies:
        copy.start()
    return copies


def wait(copies):
    for copy in copies:
        copy.wait()


def eigen_values(first, width):
    column = iota((1, width), 1) + first
    wave = jnp.where(column < HALF, 2 * column + 1, 2 * column + 2 - N).astype(jnp.float32)
    angle = wave * (math.pi / (2 * (N + 1)))
    square = angle * angle
    series = jnp.full_like(square, 1.0 / math.factorial(15))
    for order in (13, 11, 9, 7, 5, 3, 1):
        series = 1.0 / math.factorial(order) - square * series
    sine = angle * series
    return 4.0 * sine * sine


def radii_column(radii_ref, shape):
    sub = iota(shape, 0)
    column = jnp.zeros(shape, jnp.float32)
    for m in range(NL):
        column = jnp.where(sub == m, radii_ref[m], column)
    return column


def decay_of(shift):
    half = 0.5 * jnp.sqrt(shift)
    root = jnp.sqrt(1.0 + 0.25 * shift)
    grow = half + root
    return 1.0 / (grow * grow), 1.0 / (4.0 * half * root)


def mode_decay(radii_ref):
    return decay_of(eigen_values(0, N) + radii_column(radii_ref, (NL, N)))


def forward_kernel(
    vortex_hbm, mix_hbm, back_hbm, radii_hbm, wave_hbm,
    send_hbm, carry_hbm,
    vortex_ref, mix_ref, back_ref, radii_ref, wave_ref, table_ref, send_ref, force_ref, sems,
):
    copies = fetch([(mix_hbm, mix_ref), (radii_hbm, radii_ref)], sems)
    waves = fetch([(wave_hbm.at[i], wave_ref.at[i]) for i in range(2)], sems, 7)
    layers = [pl.ds(i, 4) for i in range(0, NL, 4)]
    loads = fetch([(vortex_hbm.at[some], vortex_ref.at[some]) for some in layers], sems, 2)
    copies += fetch([(back_hbm, back_ref)], sems, 6)

    def build(odd):
        for a in range(16):
            block = wave_ref[odd, 0, a : a + 1] * wave_ref[odd, 2]
            block += wave_ref[odd, 0, 16 + a : 17 + a] * wave_ref[odd, 1]
            high, low = halves(block)
            table_ref[odd, 0, 32 * a : 32 * a + 32] = high
            table_ref[odd, 1, 32 * a : 32 * a + 32] = low

    rows = NL * ROWS
    spread = (iota((NL, rows), 1) // ROWS == iota((NL, rows), 0)).astype(jnp.float32)
    wait(copies[:2])
    rho, weight = mode_decay(radii_ref)
    force_ref[2 * ROWS : 2 * ROWS + 2] = rho.reshape(2, ROWS, N)
    wide = dot(mix_ref[...], spread, HIGHEST)
    mix = jnp.concatenate([wide] * ROWS, 0)
    mix = jnp.where(iota((rows, rows), 0) // NL == iota((rows, rows), 1) % ROWS, mix, 0.0)
    waves[0].wait()
    build(0)
    wait(loads + waves[1:])
    written = fetch([(vortex_ref, carry_hbm.at[pl.ds(2 * TALL, NL)])], sems, 16 + PIECES)
    high, low = halves(mix)
    mix = jnp.concatenate([jnp.concatenate([high, high], 1), jnp.concatenate([low, jnp.zeros_like(low)], 1)], 0)
    modal = dot(mix, jnp.concatenate(halves(vortex_ref[...].reshape(rows, N)), 0))
    modal = modal[:rows] + modal[rows:]
    wait(copies[2:])
    force_ref[2 * ROWS + 2 :, :, :NL] = back_ref[...].reshape(2, ROWS, NL)
    rest = pl.ds(2 * ROWS, 4)
    written += fetch([(force_ref.at[rest], carry_hbm.at[rest])], sems, 15 + PIECES)
    mirror = mirrored(modal[:, HALF:])
    folded = [halves(modal[:, :HALF] + mirror), halves(modal[:, :HALF] - mirror)]
    for n in range(PIECES):
        cols = slice(n * STEP, (n + 1) * STEP)
        odd, start = divmod(n * STEP, HALF)
        if odd and start == 0:
            build(1)
        some = slice(start, start + STEP)
        spectrum = split_dot(folded[odd], (table_ref[odd, 0, :, some], table_ref[odd, 1, :, some]))
        right = jnp.zeros((NL, STEP), jnp.float32)
        left = jnp.zeros((NL, STEP), jnp.float32)
        force = []
        for y in range(ROWS):
            force.append(-weight[:, cols] * spectrum[y * NL : (y + 1) * NL])
            force_ref[2 * y : 2 * y + 2, :, cols] = force[y].reshape(2, ROWS, STEP)
            right = rho[:, cols] * right + force[y]
        for y in reversed(range(ROWS)):
            left = rho[:, cols] * left + force[y]
        for c in range(STEP // LANES):
            dest = n * (STEP // LANES) + c
            part = slice(c * LANES, (c + 1) * LANES)
            send_ref[dest * NL : (dest + 1) * NL, 0, :LANES] = right[:, part]
            send_ref[dest * NL : (dest + 1) * NL, 0, LANES : 2 * LANES] = left[:, part]
            part = slice(dest * LANES, (dest + 1) * LANES)
            send_ref[dest * NL : (dest + 1) * NL, 0, 2 * LANES : 3 * LANES] = vortex_ref[:, ROWS - 1, part]
            send_ref[dest * NL : (dest + 1) * NL, 0, 3 * LANES :] = vortex_ref[:, 0, part]
        dests = pl.ds(n * (STEP // LANES) * NL, STEP // LANES * NL)
        written += fetch([(send_ref.at[dests], send_hbm.at[dests])], sems, 15 + n)
        some = pl.ds(0, 2 * ROWS), slice(None), pl.ds(n * STEP, STEP)
        written += fetch([(force_ref.at[some], carry_hbm.at[some])], sems, 17 + PIECES + n)
    wait(written)


def shift_rows(value, step):
    blank = jnp.zeros((abs(step), value.shape[1]), value.dtype)
    if step > 0:
        return jnp.concatenate([blank, value[:-step]], 0)
    return jnp.concatenate([value[-step:], blank], 0)


def scan_kernel(take_ref, ends_ref, give_hbm, give_ref, sems):
    rates = [ends_ref[2 * BLOCKS + bit : 2 * BLOCKS + bit + 1] for bit in range(8)]
    rho = ends_ref[2 * BLOCKS + 8 : 2 * BLOCKS + 9]
    right = take_ref[:, 0, :LANES]
    left = take_ref[:, 0, LANES : 2 * LANES]
    for bit, rate in enumerate(rates[:-1]):
        right = right + rate * shift_rows(right, 1 << bit)
        left = left + rate * shift_rows(left, -1 << bit)
    below = rho * left[:1]
    above = rho * right[BLOCKS - 1 :]
    far = rates[-1] * rho
    scale = 1.0 / (1.0 - far * far)
    alpha = -(below - far * above) * scale
    beta = -(above - far * below) * scale
    give_ref[:, 0, :LANES] = shift_rows(right, 1) + alpha * ends_ref[:BLOCKS]
    give_ref[:, 0, LANES : 2 * LANES] = shift_rows(left, -1) + beta * ends_ref[BLOCKS : 2 * BLOCKS]
    give_ref[:, 0, 2 * LANES : 3 * LANES] = shift_rows(take_ref[:, 0, 2 * LANES : 3 * LANES], 1)
    give_ref[:, 0, 3 * LANES :] = shift_rows(take_ref[:, 0, 3 * LANES :], -1)
    wait(fetch([(give_ref, give_hbm)], sems))


def part_kernel(
    index_ref, carry_hbm, part_ref, mixed_ref, ends_ref, force_ref, sems
):
    wait(fetch([(carry_hbm.at[pl.ds(0, 2 * TALL)], force_ref)], sems))
    me = index_ref[0]
    here = pl.ds(pl.multiple_of(me // NL * LANES, LANES), LANES)
    every = force_ref[2 * ROWS : 2 * ROWS + 2, :, here].reshape(NL, LANES)
    rho = jnp.sum(jnp.where(iota((NL, LANES), 0) == me % NL, every, 0.0), 0, keepdims=True)
    rate = rho
    for _ in range(3):
        rate = rate * rate
    place = iota((BLOCKS, LANES), 0)
    power = jnp.ones((BLOCKS, LANES), jnp.float32)
    reverse = power
    for bit in range(8):
        ends_ref[2 * BLOCKS + bit : 2 * BLOCKS + bit + 1] = rate
        if bit < 7:
            odd = (place >> bit) % 2 == 1
            power = power * jnp.where(odd, rate, 1.0)
            reverse = reverse * jnp.where(odd, 1.0, rate)
        rate = rate * rate
    ends_ref[2 * BLOCKS + 8 : 2 * BLOCKS + 9] = rho
    ends_ref[:BLOCKS] = power
    ends_ref[BLOCKS : 2 * BLOCKS] = reverse
    tall = NL * TALL
    row = iota((tall, NL), 0)
    layer = jnp.where(row < NL * ROWS, row // ROWS, row % NL)
    pick = (layer == iota((tall, NL), 1)).astype(jnp.float32)
    wide = (iota((NL, tall), 1) % NL == iota((NL, tall), 0)).astype(jnp.float32)
    mixed = dot(dot(pick, force_ref[2 * ROWS + 2 :, :, :NL].reshape(NL, NL), HIGHEST), wide, HIGHEST)
    row = iota((tall, tall), 0)
    place = jnp.where(row < NL * ROWS, row % ROWS + 1, jnp.where(row < NL * (ROWS + 1), 0, ROWS + 1))
    mixed_ref[...] = jnp.where(iota((tall, tall), 1) // NL == place, mixed, 0.0)
    force = [force_ref[2 * y : 2 * y + 2].reshape(NL, N) for y in range(ROWS + 1)]
    rho = force[ROWS]
    part_ref[TALL] = rho
    right = jnp.zeros((NL, N), jnp.float32)
    for y in range(ROWS):
        right = rho * right + force[y]
        part_ref[y + 1] = right
    part_ref[ROWS + 1] = rho * right
    left = jnp.zeros((NL, N), jnp.float32)
    for y in reversed(range(ROWS)):
        part_ref[y + 1] += left
        left = rho * (left + force[y])
    part_ref[0] = left


def roll_lanes(value, step):
    width = value.shape[1]
    rolled = pltpu.roll(value, step % width, 1)
    lane = iota((value.shape[0], LANES), 1)
    if step > 0:
        edge = jnp.where(lane == 0, 0.0, rolled[:, :LANES])
        return jnp.concatenate([edge, rolled[:, LANES:]], 1)
    edge = jnp.where(lane == LANES - 1, 0.0, rolled[:, -LANES:])
    return jnp.concatenate([rolled[:, :-LANES], edge], 1)


def roll_sub(value, edge, step):
    height = value.shape[0]
    sub = iota(value.shape, 0)
    rolled = pltpu.roll(value, step % height, 0)
    return jnp.where(sub == (0 if step > 0 else height - 1), edge, rolled)


def difference(value):
    return roll_lanes(value, -1) - roll_lanes(value, 1)


def backward_kernel(
    index_ref, take_ref, part_ref, mixed_ref, table_ref, wet_ref, wind_ref, carry_hbm, vortex_hbm, stream_hbm, given_ref, psi_ref,
    south_ref, north_ref, edge_ref, wave_ref, vortex_ref, stream_ref, sems,
):
    loads = fetch(
        [(carry_hbm.at[pl.ds(2 * TALL + i, 4)], given_ref.at[pl.ds(i, 4)]) for i in range(0, NL, 4)], sems
    )
    out = len(loads)
    for c in range(N // LANES):
        cols = slice(c * LANES, (c + 1) * LANES)
        up = take_ref[c * NL : (c + 1) * NL, 0, :LANES]
        down = take_ref[c * NL : (c + 1) * NL, 0, LANES : 2 * LANES]
        south_ref[:, cols] = take_ref[c * NL : (c + 1) * NL, 0, 2 * LANES : 3 * LANES]
        north_ref[:, cols] = take_ref[c * NL : (c + 1) * NL, 0, 3 * LANES :]
        near = part_ref[TALL, :, cols]
        ups, downs = [up], [down]
        for _ in range(ROWS + 1):
            ups.append(ups[-1] * near)
            downs.append(downs[-1] * near)
        for i in range(TALL):
            psi_ref[i * NL : (i + 1) * NL, cols] = part_ref[i, :, cols] + ups[i] + downs[ROWS + 1 - i]
    split = halves(dot(mixed_ref[...], psi_ref[...], HIGHEST))
    sums = []
    for odd in range(2):
        some = tuple(part[:, odd * HALF : (odd + 1) * HALF] for part in split)
        sums.append(split_dot(some, (table_ref[odd, 0], table_ref[odd, 1]), 1))
    wave_ref[:, :HALF] = sums[0] + sums[1]
    wave_ref[:, HALF:] = mirrored(sums[0] - sums[1], True)
    inside_low = jnp.where(index_ref[0] > 0, 1.0, 0.0)
    inside_high = jnp.where(index_ref[0] < BLOCKS - 1, 1.0, 0.0)
    body = NL * ROWS
    for layer in range(NL):
        stream_ref[layer] = wave_ref[layer * ROWS : (layer + 1) * ROWS]
    written = fetch([(stream_ref, stream_hbm)], sems, out)
    wait(loads)
    keep = time_step * wet_ref[...].astype(jnp.float32)
    twelfth = keep * (1.0 / 12.0)
    streams = inside_low * wave_ref[body : body + NL], inside_high * wave_ref[body + NL :]
    for side, (stream, old) in enumerate(zip(streams, (south_ref[...], north_ref[...]))):
        edge_ref[3 * side] = stream
        edge_ref[3 * side + 1] = old
        edge_ref[3 * side + 2] = difference(old) * stream - old * difference(stream)
    for layer in range(NL):
        rows = [edge_ref[i, layer : layer + 1] for i in range(6)]

        def rise(value, i):
            return roll_sub(value, rows[3 + i], -1) - roll_sub(value, rows[i], 1)

        mid = stream_ref[layer]
        old = given_ref[layer]
        east, west = roll_lanes(mid, -1), roll_lanes(mid, 1)
        across, along = east - west, rise(mid, 0)
        old_across, old_along = difference(old), rise(old, 1)
        total = old_across * along - old_along * across
        total += rise(old_across * mid - old * across, 2)
        total -= difference((old_along + 12.0 * 0.5 * beta_plane) * mid - old * along)
        total = old + twelfth * total
        if layer == 0:
            total += keep * wind_ref[...]
        if layer == NL - 1:
            both = roll_sub(mid, rows[3], -1) + roll_sub(mid, rows[0], 1)
            total -= (bottom_drag * keep) * (both + east + west - 4.0 * mid)
        vortex_ref[layer] = total
        if layer % 4 == 3:
            some = slice(layer - 3, layer + 1)
            written += fetch([(vortex_ref.at[some], vortex_hbm.at[some])], sems, out + 1 + layer // 4)
    wait(written)


def call(kernel, outs, args, scratch, flops, nbytes, scalars=(), near=(), limit=60 * 1024 * 1024, kept=0):
    def room(kind):
        return pltpu.VMEM(*kind) if isinstance(kind, tuple) else kind

    return pl.pallas_call(
        kernel,
        out_shape=[jax.ShapeDtypeStruct(s, d) for s, d in outs],
        in_specs=[SMEM] * len(scalars) + [VMEM] * len(near) + [ANY] * len(args),
        out_specs=[ANY] * (len(outs) - kept) + [VMEM] * kept,
        scratch_shapes=[room(kind) for kind in scratch],
        compiler_params=pltpu.CompilerParams(vmem_limit_bytes=limit),
        cost_estimate=pl.CostEstimate(flops=flops, bytes_accessed=nbytes, transcendentals=0),
    )(*scalars, *near, *args)


def body(vorticity, layer_to_mode, mode_to_layer, inverse_radii, wind_curl, wet_mask):
    field = ((NL, ROWS, N), f32)
    plane = ((ROWS, N), f32)
    edge = ((NL, N), f32)
    mixing = ((NL, NL), f32)
    sines = ((2, 2, HALF, HALF), bf16)
    packet = ((BLOCKS, 1, 4 * LANES), f32)
    rows = ((2 * TALL, ROWS, N), f32)
    carry = ((112, ROWS, N), f32)
    rates = pltpu.SMEM((NL,), f32)
    parts = [((TALL + 1, NL, N), f32), ((NL * TALL, NL * TALL), f32)]
    ends = ((2 * BLOCKS + 16, LANES), f32)
    wave = ((NL * TALL, N), f32)

    index = (lax.axis_index("group") * lax.axis_size("tile") + lax.axis_index("tile")).astype(i32).reshape(1)
    outs = [packet, carry]
    table = jnp.asarray(host_table())
    send, kept = call(
        forward_kernel, outs, (vorticity, layer_to_mode, mode_to_layer, inverse_radii, jnp.asarray(host_waves())),
        [field, mixing, mixing, rates, ((2, 3, 32, HALF), f32), sines, packet, rows, DMA((17 + 2 * PIECES,))],
        6 * 128 * N * N, 6 << 20, limit=64000 << 10,
    )
    take = lax.all_to_all(send, AXES, split_axis=0, concat_axis=0, tiled=True)
    part, mixed, ends = call(
        part_kernel, [*parts, ends], (kept,), [rows, DMA((1,))], 1 << 24, 1 << 20, [index], limit=50000 << 10, kept=3
    )
    (give,) = call(
        scan_kernel, [packet], (), [packet, DMA((1,))], 1 << 22, 1 << 18, (), [take, ends], limit=54500 << 10,
    )
    amplitude = lax.all_to_all(give, AXES, split_axis=0, concat_axis=0, tiled=True)
    return tuple(
        call(
            backward_kernel, [field, field],
            (kept,), [field, wave, edge, edge, ((6, NL, N), f32), wave, field, field, DMA((9,))],
            6 * 160 * N * N, 6 << 20, [index], [amplitude, part, mixed, table, wet_mask, wind_curl], limit=51500 << 10,
        )
    )


def solution(mesh):
    rows = P(None, AXES, None)
    return jax.shard_map(
        body,
        mesh=mesh,
        in_specs=(rows, P(), P(), P(), P(AXES, None), P(AXES, None)),
        out_specs=(rows, rows),
        check_vma=False,
    )
```

```python
import math

import jax
import jax.numpy as jnp
import numpy as np
from jax import lax
from jax.experimental import pallas as pl
from jax.experimental.pallas import tpu as pltpu
from jax.sharding import PartitionSpec as P

time_step = 0.5
beta_plane = 1.0
bottom_drag = 0.2

N = 1024
NL = 16
ROWS = 8
TALL = ROWS + 2
BLOCKS = 128
LANES = 128
HALF = N // 2
STEP = 256
PIECES = N // STEP
AXES = ("group", "tile")
HIGHEST = lax.Precision.HIGHEST
SMEM = pl.BlockSpec(memory_space=pltpu.SMEM)
VMEM = pl.BlockSpec(memory_space=pltpu.VMEM)
ANY = pl.BlockSpec(memory_space=pl.ANY)
DMA = pltpu.SemaphoreType.DMA
f32, bf16, i32 = jnp.float32, jnp.bfloat16, jnp.int32


def host_table():
    k = np.arange(1, N + 1)
    sine = math.sqrt(2.0 / (N + 1)) * np.sin(np.pi * ((k[:, None] * k[None, :]) % (2 * (N + 1))) / (N + 1))
    table = np.stack([sine[:HALF, 0::2], sine[:HALF, 1::2]])
    high = table.astype(jnp.bfloat16)
    low = (table - high.astype(np.float64)).astype(jnp.bfloat16)
    return np.stack([high, low], 1)


def host_waves():
    found = []
    for odd in range(2):
        wave = np.arange(1 + odd, N + 1, 2)
        angle_a, angle_b = (
            np.pi * ((place[:, None] * wave[None, :]) % (2 * (N + 1))) / (N + 1)
            for place in (32 * np.arange(16), np.arange(1, 33))
        )
        scale = math.sqrt(2.0 / (N + 1))
        rows = [np.sin(angle_a), np.cos(angle_a), scale * np.sin(angle_b), scale * np.cos(angle_b)]
        found.append(np.concatenate(rows, 0).reshape(3, 32, HALF))
    return np.stack(found).astype(np.float32)


def iota(shape, dim):
    return lax.broadcasted_iota(jnp.int32, shape, dim)


def dot(left, right, precision=None, across=0):
    return lax.dot_general(
        left, right, (((1,), (across,)), ((), ())), precision=precision, preferred_element_type=jnp.float32
    )


def halves(value):
    high = value.astype(jnp.bfloat16)
    low = (value - high.astype(jnp.float32)).astype(jnp.bfloat16)
    return high, low


def split_dot(left, right, across=0):
    count = left[0].shape[0]
    both = dot(jnp.concatenate(left, 0), right[0], None, across)
    return both[:count] + both[count:] + dot(left[0], right[1], None, across)


def mirrored(value, third=False):
    flip = (iota((STEP, STEP), 0) + iota((STEP, STEP), 1) == STEP - 1).astype(jnp.bfloat16)
    count, width = value.shape
    parts = list(halves(value))
    if third:
        rest = value - parts[0].astype(jnp.float32) - parts[1].astype(jnp.float32)
        parts.append(rest.astype(jnp.bfloat16))
    stack = jnp.concatenate(parts, 0)
    blocks = []
    for i in reversed(range(0, width, STEP)):
        block = dot(stack[:, i : i + STEP], flip)
        blocks.append(sum(block[j * count : (j + 1) * count] for j in reversed(range(len(parts)))))
    return jnp.concatenate(blocks, 1)


def fetch(pairs, sems, first=0):
    copies = [pltpu.make_async_copy(src, dst, sems.at[first + i]) for i, (src, dst) in enumerate(pairs)]
    for copy in copies:
        copy.start()
    return copies


def wait(copies):
    for copy in copies:
        copy.wait()


def eigen_values(first, width):
    column = iota((1, width), 1) + first
    wave = jnp.where(column < HALF, 2 * column + 1, 2 * column + 2 - N).astype(jnp.float32)
    angle = wave * (math.pi / (2 * (N + 1)))
    square = angle * angle
    series = jnp.full_like(square, 1.0 / math.factorial(15))
    for order in (13, 11, 9, 7, 5, 3, 1):
        series = 1.0 / math.factorial(order) - square * series
    sine = angle * series
    return 4.0 * sine * sine


def radii_column(radii_ref, shape):
    sub = iota(shape, 0)
    column = jnp.zeros(shape, jnp.float32)
    for m in range(NL):
        column = jnp.where(sub == m, radii_ref[m], column)
    return column


def decay_of(shift):
    half = 0.5 * jnp.sqrt(shift)
    root = jnp.sqrt(1.0 + 0.25 * shift)
    grow = half + root
    return 1.0 / (grow * grow), 1.0 / (4.0 * half * root)


def mode_decay(radii_ref):
    return decay_of(eigen_values(0, N) + radii_column(radii_ref, (NL, N)))


def forward_kernel(
    vortex_hbm, mix_hbm, back_hbm, radii_hbm, wave_hbm,
    send_hbm, carry_hbm,
    vortex_ref, mix_ref, back_ref, radii_ref, wave_ref, table_ref, send_ref, force_ref, sems,
):
    copies = fetch([(mix_hbm, mix_ref), (radii_hbm, radii_ref)], sems)
    waves = fetch([(wave_hbm.at[i], wave_ref.at[i]) for i in range(2)], sems, 7)
    layers = [pl.ds(i, 4) for i in range(0, NL, 4)]
    loads = fetch([(vortex_hbm.at[some], vortex_ref.at[some]) for some in layers], sems, 2)
    copies += fetch([(back_hbm, back_ref)], sems, 6)

    def build(odd):
        for a in range(16):
            block = wave_ref[odd, 0, a : a + 1] * wave_ref[odd, 2]
            block += wave_ref[odd, 0, 16 + a : 17 + a] * wave_ref[odd, 1]
            high, low = halves(block)
            table_ref[odd, 0, 32 * a : 32 * a + 32] = high
            table_ref[odd, 1, 32 * a : 32 * a + 32] = low

    rows = NL * ROWS
    spread = (iota((NL, rows), 1) // ROWS == iota((NL, rows), 0)).astype(jnp.float32)
    wait(copies[:2])
    rho, weight = mode_decay(radii_ref)
    force_ref[2 * ROWS : 2 * ROWS + 2] = rho.reshape(2, ROWS, N)
    wide = dot(mix_ref[...], spread, HIGHEST)
    mix = jnp.concatenate([wide] * ROWS, 0)
    mix = jnp.where(iota((rows, rows), 0) // NL == iota((rows, rows), 1) % ROWS, mix, 0.0)
    waves[0].wait()
    build(0)
    wait(loads + waves[1:])
    written = fetch([(vortex_ref, carry_hbm.at[pl.ds(2 * TALL, NL)])], sems, 16 + PIECES)
    high, low = halves(mix)
    mix = jnp.concatenate([jnp.concatenate([high, high], 1), jnp.concatenate([low, jnp.zeros_like(low)], 1)], 0)
    modal = dot(mix, jnp.concatenate(halves(vortex_ref[...].reshape(rows, N)), 0))
    modal = modal[:rows] + modal[rows:]
    wait(copies[2:])
    force_ref[2 * ROWS + 2 :, :, :NL] = back_ref[...].reshape(2, ROWS, NL)
    rest = pl.ds(2 * ROWS, 4)
    written += fetch([(force_ref.at[rest], carry_hbm.at[rest])], sems, 15 + PIECES)
    mirror = mirrored(modal[:, HALF:])
    folded = [halves(modal[:, :HALF] + mirror), halves(modal[:, :HALF] - mirror)]
    for n in range(PIECES):
        cols = slice(n * STEP, (n + 1) * STEP)
        odd, start = divmod(n * STEP, HALF)
        if odd and start == 0:
            build(1)
        some = slice(start, start + STEP)
        spectrum = split_dot(folded[odd], (table_ref[odd, 0, :, some], table_ref[odd, 1, :, some]))
        right = jnp.zeros((NL, STEP), jnp.float32)
        left = jnp.zeros((NL, STEP), jnp.float32)
        force = []
        for y in range(ROWS):
            force.append(-weight[:, cols] * spectrum[y * NL : (y + 1) * NL])
            force_ref[2 * y : 2 * y + 2, :, cols] = force[y].reshape(2, ROWS, STEP)
            right = rho[:, cols] * right + force[y]
        for y in reversed(range(ROWS)):
            left = rho[:, cols] * left + force[y]
        for c in range(STEP // LANES):
            dest = n * (STEP // LANES) + c
            part = slice(c * LANES, (c + 1) * LANES)
            send_ref[dest * NL : (dest + 1) * NL, 0, :LANES] = right[:, part]
            send_ref[dest * NL : (dest + 1) * NL, 0, LANES : 2 * LANES] = left[:, part]
            part = slice(dest * LANES, (dest + 1) * LANES)
            send_ref[dest * NL : (dest + 1) * NL, 0, 2 * LANES : 3 * LANES] = vortex_ref[:, ROWS - 1, part]
            send_ref[dest * NL : (dest + 1) * NL, 0, 3 * LANES :] = vortex_ref[:, 0, part]
        dests = pl.ds(n * (STEP // LANES) * NL, STEP // LANES * NL)
        written += fetch([(send_ref.at[dests], send_hbm.at[dests])], sems, 15 + n)
        some = pl.ds(0, 2 * ROWS), slice(None), pl.ds(n * STEP, STEP)
        written += fetch([(force_ref.at[some], carry_hbm.at[some])], sems, 17 + PIECES + n)
    wait(written)


def shift_rows(value, step):
    blank = jnp.zeros((abs(step), value.shape[1]), value.dtype)
    if step > 0:
        return jnp.concatenate([blank, value[:-step]], 0)
    return jnp.concatenate([value[-step:], blank], 0)


def scan_kernel(take_ref, ends_ref, give_hbm, give_ref, sems):
    rates = [ends_ref[2 * BLOCKS + bit : 2 * BLOCKS + bit + 1] for bit in range(8)]
    rho = ends_ref[2 * BLOCKS + 8 : 2 * BLOCKS + 9]
    right = take_ref[:, 0, :LANES]
    left = take_ref[:, 0, LANES : 2 * LANES]
    for bit, rate in enumerate(rates[:-1]):
        right = right + rate * shift_rows(right, 1 << bit)
        left = left + rate * shift_rows(left, -1 << bit)
    below = rho * left[:1]
    above = rho * right[BLOCKS - 1 :]
    far = rates[-1] * rho
    scale = 1.0 / (1.0 - far * far)
    alpha = -(below - far * above) * scale
    beta = -(above - far * below) * scale
    give_ref[:, 0, :LANES] = shift_rows(right, 1) + alpha * ends_ref[:BLOCKS]
    give_ref[:, 0, LANES : 2 * LANES] = shift_rows(left, -1) + beta * ends_ref[BLOCKS : 2 * BLOCKS]
    give_ref[:, 0, 2 * LANES : 3 * LANES] = shift_rows(take_ref[:, 0, 2 * LANES : 3 * LANES], 1)
    give_ref[:, 0, 3 * LANES :] = shift_rows(take_ref[:, 0, 3 * LANES :], -1)
    wait(fetch([(give_ref, give_hbm)], sems))


def part_kernel(
    index_ref, carry_hbm, part_ref, mixed_ref, ends_ref, force_ref, sems
):
    wait(fetch([(carry_hbm.at[pl.ds(0, 2 * TALL)], force_ref)], sems))
    me = index_ref[0]
    here = pl.ds(pl.multiple_of(me // NL * LANES, LANES), LANES)
    every = force_ref[2 * ROWS : 2 * ROWS + 2, :, here].reshape(NL, LANES)
    rho = jnp.sum(jnp.where(iota((NL, LANES), 0) == me % NL, every, 0.0), 0, keepdims=True)
    rate = rho
    for _ in range(3):
        rate = rate * rate
    place = iota((BLOCKS, LANES), 0)
    power = jnp.ones((BLOCKS, LANES), jnp.float32)
    reverse = power
    for bit in range(8):
        ends_ref[2 * BLOCKS + bit : 2 * BLOCKS + bit + 1] = rate
        if bit < 7:
            odd = (place >> bit) % 2 == 1
            power = power * jnp.where(odd, rate, 1.0)
            reverse = reverse * jnp.where(odd, 1.0, rate)
        rate = rate * rate
    ends_ref[2 * BLOCKS + 8 : 2 * BLOCKS + 9] = rho
    ends_ref[:BLOCKS] = power
    ends_ref[BLOCKS : 2 * BLOCKS] = reverse
    tall = NL * TALL
    row = iota((tall, NL), 0)
    layer = jnp.where(row < NL * ROWS, row // ROWS, row % NL)
    pick = (layer == iota((tall, NL), 1)).astype(jnp.float32)
    wide = (iota((NL, tall), 1) % NL == iota((NL, tall), 0)).astype(jnp.float32)
    mixed = dot(dot(pick, force_ref[2 * ROWS + 2 :, :, :NL].reshape(NL, NL), HIGHEST), wide, HIGHEST)
    row = iota((tall, tall), 0)
    place = jnp.where(row < NL * ROWS, row % ROWS + 1, jnp.where(row < NL * (ROWS + 1), 0, ROWS + 1))
    mixed_ref[...] = jnp.where(iota((tall, tall), 1) // NL == place, mixed, 0.0)
    force = [force_ref[2 * y : 2 * y + 2].reshape(NL, N) for y in range(ROWS + 1)]
    rho = force[ROWS]
    part_ref[TALL] = rho
    right = jnp.zeros((NL, N), jnp.float32)
    for y in range(ROWS):
        right = rho * right + force[y]
        part_ref[y + 1] = right
    part_ref[ROWS + 1] = rho * right
    left = jnp.zeros((NL, N), jnp.float32)
    for y in reversed(range(ROWS)):
        part_ref[y + 1] += left
        left = rho * (left + force[y])
    part_ref[0] = left


def roll_lanes(value, step):
    width = value.shape[1]
    rolled = pltpu.roll(value, step % width, 1)
    lane = iota((value.shape[0], LANES), 1)
    if step > 0:
        edge = jnp.where(lane == 0, 0.0, rolled[:, :LANES])
        return jnp.concatenate([edge, rolled[:, LANES:]], 1)
    edge = jnp.where(lane == LANES - 1, 0.0, rolled[:, -LANES:])
    return jnp.concatenate([rolled[:, :-LANES], edge], 1)


def roll_sub(value, edge, step):
    height = value.shape[0]
    sub = iota(value.shape, 0)
    rolled = pltpu.roll(value, step % height, 0)
    return jnp.where(sub == (0 if step > 0 else height - 1), edge, rolled)


def difference(value):
    return roll_lanes(value, -1) - roll_lanes(value, 1)


def backward_kernel(
    index_ref, take_ref, part_ref, mixed_ref, table_ref, wet_ref, wind_ref, carry_hbm, vortex_hbm, stream_hbm, given_ref, psi_ref,
    south_ref, north_ref, edge_ref, wave_ref, vortex_ref, stream_ref, sems,
):
    loads = fetch(
        [(carry_hbm.at[pl.ds(2 * TALL + i, 4)], given_ref.at[pl.ds(i, 4)]) for i in range(0, NL, 4)], sems
    )
    out = len(loads)
    for c in range(N // LANES):
        cols = slice(c * LANES, (c + 1) * LANES)
        up = take_ref[c * NL : (c + 1) * NL, 0, :LANES]
        down = take_ref[c * NL : (c + 1) * NL, 0, LANES : 2 * LANES]
        south_ref[:, cols] = take_ref[c * NL : (c + 1) * NL, 0, 2 * LANES : 3 * LANES]
        north_ref[:, cols] = take_ref[c * NL : (c + 1) * NL, 0, 3 * LANES :]
        near = part_ref[TALL, :, cols]
        ups, downs = [up], [down]
        for _ in range(ROWS + 1):
            ups.append(ups[-1] * near)
            downs.append(downs[-1] * near)
        for i in range(TALL):
            psi_ref[i * NL : (i + 1) * NL, cols] = part_ref[i, :, cols] + ups[i] + downs[ROWS + 1 - i]
    split = halves(dot(mixed_ref[...], psi_ref[...], HIGHEST))
    sums = []
    for odd in range(2):
        some = tuple(part[:, odd * HALF : (odd + 1) * HALF] for part in split)
        sums.append(split_dot(some, (table_ref[odd, 0], table_ref[odd, 1]), 1))
    wave_ref[:, :HALF] = sums[0] + sums[1]
    wave_ref[:, HALF:] = mirrored(sums[0] - sums[1], True)
    inside_low = jnp.where(index_ref[0] > 0, 1.0, 0.0)
    inside_high = jnp.where(index_ref[0] < BLOCKS - 1, 1.0, 0.0)
    body = NL * ROWS
    for layer in range(NL):
        stream_ref[layer] = wave_ref[layer * ROWS : (layer + 1) * ROWS]
    written = fetch([(stream_ref, stream_hbm)], sems, out)
    wait(loads)
    keep = time_step * wet_ref[...].astype(jnp.float32)
    twelfth = keep * (1.0 / 12.0)
    streams = inside_low * wave_ref[body : body + NL], inside_high * wave_ref[body + NL :]
    for side, (stream, old) in enumerate(zip(streams, (south_ref[...], north_ref[...]))):
        edge_ref[3 * side] = stream
        edge_ref[3 * side + 1] = old
        edge_ref[3 * side + 2] = difference(old) * stream - old * difference(stream)
    for layer in range(NL):
        rows = [edge_ref[i, layer : layer + 1] for i in range(6)]

        def rise(value, i):
            return roll_sub(value, rows[3 + i], -1) - roll_sub(value, rows[i], 1)

        mid = stream_ref[layer]
        old = given_ref[layer]
        east, west = roll_lanes(mid, -1), roll_lanes(mid, 1)
        across, along = east - west, rise(mid, 0)
        old_across, old_along = difference(old), rise(old, 1)
        total = old_across * along - old_along * across
        total += rise(old_across * mid - old * across, 2)
        total -= difference((old_along + 12.0 * 0.5 * beta_plane) * mid - old * along)
        total = old + twelfth * total
        if layer == 0:
            total += keep * wind_ref[...]
        if layer == NL - 1:
            both = roll_sub(mid, rows[3], -1) + roll_sub(mid, rows[0], 1)
            total -= (bottom_drag * keep) * (both + east + west - 4.0 * mid)
        vortex_ref[layer] = total
        if layer % 2 == 1:
            some = slice(layer - 1, layer + 1)
            written += fetch([(vortex_ref.at[some], vortex_hbm.at[some])], sems, out + 1 + layer // 2)
    wait(written)


def call(kernel, outs, args, scratch, flops, nbytes, scalars=(), near=(), limit=60 * 1024 * 1024, kept=0):
    def room(kind):
        return pltpu.VMEM(*kind) if isinstance(kind, tuple) else kind

    return pl.pallas_call(
        kernel,
        out_shape=[jax.ShapeDtypeStruct(s, d) for s, d in outs],
        in_specs=[SMEM] * len(scalars) + [VMEM] * len(near) + [ANY] * len(args),
        out_specs=[ANY] * (len(outs) - kept) + [VMEM] * kept,
        scratch_shapes=[room(kind) for kind in scratch],
        compiler_params=pltpu.CompilerParams(vmem_limit_bytes=limit),
        cost_estimate=pl.CostEstimate(flops=flops, bytes_accessed=nbytes, transcendentals=0),
    )(*scalars, *near, *args)


def body(vorticity, layer_to_mode, mode_to_layer, inverse_radii, wind_curl, wet_mask):
    field = ((NL, ROWS, N), f32)
    plane = ((ROWS, N), f32)
    edge = ((NL, N), f32)
    mixing = ((NL, NL), f32)
    sines = ((2, 2, HALF, HALF), bf16)
    packet = ((BLOCKS, 1, 4 * LANES), f32)
    rows = ((2 * TALL, ROWS, N), f32)
    carry = ((112, ROWS, N), f32)
    rates = pltpu.SMEM((NL,), f32)
    parts = [((TALL + 1, NL, N), f32), ((NL * TALL, NL * TALL), f32)]
    ends = ((2 * BLOCKS + 16, LANES), f32)
    wave = ((NL * TALL, N), f32)

    index = (lax.axis_index("group") * lax.axis_size("tile") + lax.axis_index("tile")).astype(i32).reshape(1)
    outs = [packet, carry]
    table = jnp.asarray(host_table())
    send, kept = call(
        forward_kernel, outs, (vorticity, layer_to_mode, mode_to_layer, inverse_radii, jnp.asarray(host_waves())),
        [field, mixing, mixing, rates, ((2, 3, 32, HALF), f32), sines, packet, rows, DMA((17 + 2 * PIECES,))],
        6 * 128 * N * N, 6 << 20, limit=64000 << 10,
    )
    take = lax.all_to_all(send, AXES, split_axis=0, concat_axis=0, tiled=True)
    part, mixed, ends = call(
        part_kernel, [*parts, ends], (kept,), [rows, DMA((1,))], 1 << 24, 1 << 20, [index], limit=50000 << 10, kept=3
    )
    (give,) = call(
        scan_kernel, [packet], (), [packet, DMA((1,))], 1 << 22, 1 << 18, (), [take, ends], limit=54500 << 10,
    )
    amplitude = lax.all_to_all(give, AXES, split_axis=0, concat_axis=0, tiled=True)
    return tuple(
        call(
            backward_kernel, [field, field],
            (kept,), [field, wave, edge, edge, ((6, NL, N), f32), wave, field, field, DMA((13,))],
            6 * 160 * N * N, 6 << 20, [index], [amplitude, part, mixed, table, wet_mask, wind_curl], limit=51500 << 10,
        )
    )


def solution(mesh):
    rows = P(None, AXES, None)
    return jax.shard_map(
        body,
        mesh=mesh,
        in_specs=(rows, P(), P(), P(), P(AXES, None), P(AXES, None)),
        out_specs=(rows, rows),
        check_vma=False,
    )
```
